32 devices in a mesh: mod: 4 (over z), dp: 8 (over y, x, core).
Axes of the slice: x: 2, y: 2, z: 4, core: 2. Of those that a mesh axis runs over, the one named last changes fastest.
Arguments:
- train_grads: float32 [1024, 16, 512], P('dp', 'mod'), may hold values from -50 to 50
- queries: float32 [32, 16, 512], P('dp', 'mod'), may hold values from -6 to 6
- damping: float32 [16], P('mod'), may hold values from 0.05 to 0.5
Outputs:
- scores: float32 [1024, 32], P('dp', 'mod')
The draws below stay inside these ranges and needn't reach their ends.
All inputs are finite; a program needn't handle non-finite values.
Results may differ from the reference program's by a relative error of at most 0.012.
Values sent between devices are 32-bit elements; how exact they have to be, the bound alone decides.
No kernel may reach another device: no remote copies, remote signals or barrier semaphores. Data moves between devices by JAX's collectives and lax.ppermute only.
A program may use at most 128 MiB of HBM per device.

```python
import math
import jax
import jax.numpy as jnp
from jax import lax

PROJ_DIM = 512
NEWTON_STEPS = 8
MODULES = 16
ROWS = 1024
QUERIES = 32


def draw_train_grads(key, part):
    keys = jax.random.split(key, 3)
    spread = 1.1512925
    row_scale = jnp.exp(jax.random.uniform(keys[0], (ROWS, 1, 1), jnp.float32, -spread, spread))
    col_scale = jnp.exp(jax.random.uniform(keys[1], (1, MODULES, PROJ_DIM), jnp.float32, -spread, spread))
    base = jnp.clip(jax.random.normal(keys[2], (ROWS, MODULES, PROJ_DIM), jnp.float32), -4.0, 4.0)
    return base * row_scale * col_scale


def steps_of(rng, extent, cuts, low, high):
    factor_of, own = 1.0, jax.random.fold_in(rng, 6)
    for axis_at, shards_of in cuts:
        heights = jnp.exp(jax.random.uniform(jax.random.fold_in(own, axis_at), (shards_of,), jnp.float32, low / len(cuts), high / len(cuts)))
        factor_of = factor_of * jnp.repeat(heights, extent[axis_at] // shards_of).reshape([-1 if axis == axis_at else 1 for axis in range(len(extent))])
    return factor_of


def bell_draw(key, dims, deviation, bound, shards=(), kind=jnp.bfloat16):
    loudness = steps_of(key, dims, shards, -0.22, 0.18) if shards else 1.0
    drawn = jax.random.normal(key, dims, jnp.float32) * deviation * loudness
    return jnp.minimum(jnp.maximum(drawn, -bound), bound).astype(kind)


def setup_inputs(seed: int = 0) -> dict:
    streams_of = jax.random.split(jax.random.key(seed), 4)
    return {
        "train_grads": draw_train_grads(jax.random.fold_in(streams_of[3], 71), 0),
        "queries": bell_draw(streams_of[1], (QUERIES, MODULES, PROJ_DIM), 1.0, 6.0, ((0, 8), (1, 4)), jnp.float32),
        "damping": jnp.clip(jnp.exp(math.log(0.5) - 2.3025851 * jax.random.uniform(streams_of[2], (MODULES,), jnp.float32) ** steps_of(streams_of[2], (MODULES,), ((0, 4),), -0.2, 0.2)), 0.05, 0.5),
    }


epsilon = 1e-06

def module_term(grads_module, queries_module, damp_value):
    highest = lax.Precision.HIGHEST
    fisher = lax.dot_general(grads_module, grads_module, (((0,), (0,)), ((), ())), precision=highest, preferred_element_type=jnp.float32) / ROWS
    trace_all = jnp.trace(fisher)
    damp_shift = damp_value * trace_all / PROJ_DIM
    identity_mat = jnp.eye(PROJ_DIM, dtype=jnp.float32)
    system = fisher + damp_shift * identity_mat
    frob_norm = jnp.sqrt(jnp.sum(system * system) + epsilon)
    inverse = identity_mat / frob_norm
    for iteration in range(NEWTON_STEPS):
        product = jnp.dot(jnp.dot(inverse, system, precision=highest, preferred_element_type=jnp.float32), inverse, precision=highest, preferred_element_type=jnp.float32)
        inverse = 2.0 * inverse - product
    conditioned = jnp.dot(queries_module, inverse, precision=highest, preferred_element_type=jnp.float32)
    return lax.dot_general(grads_module, conditioned, (((1,), (1,)), ((), ())), precision=highest, preferred_element_type=jnp.float32)

def reference(train_grads, queries, damping):

    def add_module(module, running):
        grads_module = lax.dynamic_index_in_dim(train_grads, module, 1, keepdims=False)
        queries_module = lax.dynamic_index_in_dim(queries, module, 1, keepdims=False)
        damp_value = lax.dynamic_index_in_dim(damping, module, 0, keepdims=False)
        return running + module_term(grads_module, queries_module, damp_value)
    running = lax.fori_loop(0, MODULES, add_module, jnp.zeros((ROWS, QUERIES), jnp.float32))
    return running / math.sqrt(MODULES * PROJ_DIM)
```

```python
import functools
import math

import jax
import jax.numpy as jnp
from jax import lax
from jax.experimental import pallas as pl
from jax.experimental.pallas import tpu as pltpu
from jax.sharding import PartitionSpec as P

NEWTON_STEPS = 8
CORES = 2

epsilon = 1e-06

VMEM = pl.BlockSpec(memory_space=pltpu.VMEM)
SMEM = pl.BlockSpec(memory_space=pltpu.SMEM)


def halves(value):
    high = value.astype(jnp.bfloat16)
    return high, (value - high.astype(jnp.float32)).astype(jnp.bfloat16)


def product(left, right, dims=(((1,), (0,)), ((), ()))):
    return lax.dot_general(left, right, dims, preferred_element_type=jnp.float32)


def product_3(left_high, left_low, right_high, right_low, dims=(((1,), (0,)), ((), ()))):
    return (
        product(left_high, right_high, dims)
        + product(left_high, right_low, dims)
        + product(left_low, right_high, dims)
    )


def pack_kernel(offsets, rows_ref, queries_ref, *blocks):
    chip = lax.axis_index("dp") // CORES
    rows = rows_ref.shape[0]
    for offset, block in zip(offsets, blocks):
        module = lax.bitwise_xor(chip, jnp.int32(offset))
        block[0:rows] = rows_ref[:, module, :]
        block[rows:] = queries_ref[:, module, :]


def pack(offsets, train_grads, queries):
    rows, _, width = train_grads.shape
    block = jax.ShapeDtypeStruct((rows + queries.shape[0], width), jnp.float32)
    return pl.pallas_call(
        functools.partial(pack_kernel, offsets),
        out_shape=[block] * len(offsets),
        in_specs=[VMEM, VMEM],
        out_specs=[VMEM] * len(offsets),
        name="pack",
    )(train_grads, queries)


def add_gram(rows, blocks, left_ref, right_ref, stack):
    half = left_ref.shape[0]
    for place, block in enumerate(blocks):
        stack[place * rows : (place + 1) * rows] = block[0:rows]
    high, low = halves(stack[...])
    dims = (((0,), (0,)), ((), ()))
    left_ref[...] += product_3(high[:, :half], low[:, :half], high[:, :half], low[:, :half], dims)
    right_ref[...] += product_3(high, low, high[:, half:], low[:, half:], dims)


def gram_kernel(count, rows, *refs):
    blocks, refs = refs[:count], refs[count:]
    given, (left_ref, right_ref, stack) = refs[:-3], refs[-3:]
    if given:
        left_ref[...] = given[0][...]
        right_ref[...] = given[1][...]
    else:
        left_ref[...] = jnp.zeros_like(left_ref)
        right_ref[...] = jnp.zeros_like(right_ref)
    add_gram(rows, blocks, left_ref, right_ref, stack)


def gram(rows, blocks, given):
    width = blocks[0].shape[1]
    half = width // 2
    return pl.pallas_call(
        functools.partial(gram_kernel, len(blocks), rows),
        out_shape=[
            jax.ShapeDtypeStruct((half, half), jnp.float32),
            jax.ShapeDtypeStruct((width, half), jnp.float32),
        ],
        in_specs=[VMEM] * (len(blocks) + len(given)),
        out_specs=[VMEM] * 2,
        scratch_shapes=[pltpu.VMEM((len(blocks) * rows, width), jnp.float32)],
        name="gram",
    )(*blocks, *given)


def solve_kernel(sizes, *refs):
    chips, rows, per_device, groups, total_rows, scale = sizes
    refs = list(refs)
    damping_ref, left_ref, right_ref = refs[:3]
    arrived = refs[3 : 3 + chips]
    passed = refs[3 + chips : 3 + 2 * chips]
    scores = refs[3 + 2 * chips : 3 + 3 * chips]
    left, right, stack, state, high, low, asked = refs[3 + 3 * chips :]
    half = left_ref.shape[0]
    width = 2 * half
    index = lax.axis_index("dp")
    chip, core = index // CORES, index % CORES
    pair = CORES * per_device
    total_queries = chips * pair
    group = total_queries // groups
    group_here = lax.axis_index("mod")

    for offset in range(chips):
        mine = arrived[offset][rows : rows + per_device]
        other = passed[offset][rows : rows + per_device]
        both = jnp.where(
            core == 0, jnp.concatenate([mine, other], 0), jnp.concatenate([other, mine], 0)
        )
        source = lax.bitwise_xor(chip, jnp.int32(offset))
        asked[pl.ds(pl.multiple_of(source * pair, pair), pair)] = both

    left[...] = left_ref[...]
    right[...] = right_ref[...]
    add_gram(rows, passed[1:], left, right, stack)

    diagonal = lax.broadcasted_iota(jnp.int32, (half, half), 0) == lax.broadcasted_iota(
        jnp.int32, (half, half), 1
    )
    eye = diagonal.astype(jnp.float32)
    first, cross, last = left[...], right[0:half], right[half:]
    trace = jnp.sum((first + last) * eye, keepdims=True).reshape(1, 1) / total_rows
    shift = damping_ref[chip] * trace / width
    first = first / total_rows + shift * eye
    last = last / total_rows + shift * eye
    cross = cross / total_rows
    squares = first * first + last * last + 2.0 * (cross * cross)
    inverse_norm = lax.rsqrt(jnp.sum(squares, keepdims=True).reshape(1, 1) + epsilon)
    cross = cross * inverse_norm
    state[0:half, 0:half] = first * inverse_norm
    state[0:half, half:] = cross
    state[half:width, 0:half] = cross.T
    state[half:width, half:] = last * inverse_norm
    for offset in range(groups):
        source = lax.bitwise_xor(group_here, jnp.int32(offset))
        state[width + offset * group : width + (offset + 1) * group] = (
            asked[pl.ds(pl.multiple_of(source * group, group), group)] * inverse_norm
        )

    for _ in range(NEWTON_STEPS - 1):
        high[...], low[...] = halves(state[...])

        def part(start, stop, column):
            columns = slice(column, column + half)
            return product_3(
                high[start:stop],
                low[start:stop],
                high[0:width, columns],
                low[0:width, columns],
            )

        state[0:half, 0:half] = 2.0 * state[0:half, 0:half] - part(0, half, 0)
        new = 2.0 * state[0:width, half:] - part(0, width, half)
        state[0:width, half:] = new
        state[half:width, 0:half] = new[0:half].T
        state[width:, 0:half] = 2.0 * state[width:, 0:half] - part(width, width + total_queries, 0)
        state[width:, half:] = 2.0 * state[width:, half:] - part(width, width + total_queries, half)

    high[...], low[...] = halves(state[...])
    conditioned = 2.0 * state[width:] - product_3(
        high[width:], low[width:], high[0:width], low[0:width]
    )
    conditioned_high, conditioned_low = halves(conditioned * scale)
    for offset in range(chips):
        block_high, block_low = halves(arrived[offset][0:rows])
        scores[offset][...] = product_3(
            conditioned_high, conditioned_low, block_high, block_low, (((1,), (1,)), ((), ()))
        )


def solve(sizes, damping, given, arrived, passed):
    chips, rows, per_device = sizes[:3]
    width = arrived[0].shape[1]
    half = width // 2
    total_queries = chips * CORES * per_device
    return pl.pallas_call(
        functools.partial(solve_kernel, sizes),
        out_shape=[jax.ShapeDtypeStruct((total_queries, rows), jnp.float32)] * chips,
        in_specs=[SMEM] + [VMEM] * (2 + 2 * chips),
        out_specs=[VMEM] * chips,
        scratch_shapes=[
            pltpu.VMEM((half, half), jnp.float32),
            pltpu.VMEM((width, half), jnp.float32),
            pltpu.VMEM(((chips - 1) * rows, width), jnp.float32),
            pltpu.VMEM((width + total_queries, width), jnp.float32),
            pltpu.VMEM((width + total_queries, width), jnp.bfloat16),
            pltpu.VMEM((width + total_queries, width), jnp.bfloat16),
            pltpu.VMEM((total_queries, width), jnp.float32),
        ],
        name="solve",
    )(damping, *given, *arrived, *passed)


def swap(value, axis, offset):
    return lax.ppermute(value, axis, [(i, i ^ offset) for i in range(lax.axis_size(axis))])


def per_device(train_grads, queries, damping):
    rows, modules, width = train_grads.shape
    asked = queries.shape[0]
    devices = lax.axis_size("dp")
    groups = lax.axis_size("mod")
    chips = devices // CORES
    far = list(range(chips - 1, 0, -1))
    arrived = [None] * chips
    passed = [None] * chips
    packed = [None] * chips
    for offset in far + [0]:
        (packed[offset],) = pack((offset,), train_grads, queries)
    arrived[0] = packed[0]
    for offset in far:
        arrived[offset] = swap(packed[offset], "dp", offset * CORES)
    for offset in [0] + far:
        passed[offset] = swap(arrived[offset], "dp", 1)
    given = gram(rows, [arrived[0], passed[0]], ())
    given = gram(rows, [arrived[offset] for offset in far], given)
    sizes = (
        chips,
        rows,
        asked,
        groups,
        rows * devices,
        1.0 / math.sqrt(modules * groups * width),
    )
    scores = solve(sizes, damping, given, arrived, passed)
    total = scores[0]
    for offset in far:
        total = total + swap(scores[offset], "dp", offset * CORES)
    bit = groups // 2
    while bit:
        keep = total.shape[0] // 2
        total = total[:keep] + swap(total[keep:], "mod", bit)
        bit //= 2
    return total.T


def solution(mesh):
    return jax.shard_map(
        per_device,
        mesh=mesh,
        in_specs=(P("dp", "mod", None), P("dp", "mod", None), P("mod")),
        out_specs=P("dp", "mod"),
        check_vma=False,
    )
```

```python
import functools
import math

import jax
import jax.numpy as jnp
from jax import lax
from jax.experimental import pallas as pl
from jax.experimental.pallas import tpu as pltpu
from jax.sharding import PartitionSpec as P

NEWTON_STEPS = 8
CORES = 2

epsilon = 1e-06

VMEM = pl.BlockSpec(memory_space=pltpu.VMEM)
SMEM = pl.BlockSpec(memory_space=pltpu.SMEM)


def near(shape):
    return pltpu.VMEM(shape, jnp.float32)


def hold(*values):
    return [pltpu.with_memory_space_constraint(value, pltpu.VMEM) for value in values]


def grant(mebibytes):
    return pltpu.CompilerParams(vmem_limit_bytes=mebibytes << 20)


def cost(microseconds):
    return pl.CostEstimate(flops=int(microseconds * 1e9), bytes_accessed=0, transcendentals=0)


def halves(value):
    high = value.astype(jnp.bfloat16)
    return high, (value - high.astype(jnp.float32)).astype(jnp.bfloat16)


def product(left, right, dims=(((1,), (0,)), ((), ()))):
    return lax.dot_general(left, right, dims, preferred_element_type=jnp.float32)


def product_3(left_high, left_low, right_high, right_low, dims=(((1,), (0,)), ((), ()))):
    return (
        product(left_high, right_high, dims)
        + product(left_high, right_low, dims)
        + product(left_low, right_high, dims)
    )


def pack_kernel(offsets, rows_ref, queries_ref, *blocks):
    chip = lax.axis_index("dp") // CORES
    rows = rows_ref.shape[0]
    for offset, block in zip(offsets, blocks):
        module = lax.bitwise_xor(chip, jnp.int32(offset))
        block[0:rows] = rows_ref[:, module, :]
        block[rows:] = queries_ref[:, module, :]


def pack(offsets, train_grads, queries):
    rows, _, width = train_grads.shape
    block = near((rows + queries.shape[0], width))
    return pl.pallas_call(
        functools.partial(pack_kernel, offsets),
        out_shape=[block] * len(offsets),
        in_specs=[VMEM, VMEM],
        out_specs=[VMEM] * len(offsets),
        cost_estimate=cost(0.4 * len(offsets)),
        compiler_params=grant(8),
        name="pack",
    )(*hold(train_grads, queries))


def add_gram(rows, blocks, left_ref, right_ref, stack):
    half = left_ref.shape[0]
    for place, block in enumerate(blocks):
        stack[place * rows : (place + 1) * rows] = block[0:rows]
    high, low = halves(stack[...])
    dims = (((0,), (0,)), ((), ()))
    left_ref[...] += product_3(high[:, :half], low[:, :half], high[:, :half], low[:, :half], dims)
    right_ref[...] += product_3(high, low, high[:, half:], low[:, half:], dims)


def gram_kernel(count, rows, *refs):
    blocks, refs = refs[:count], refs[count:]
    given, (left_ref, right_ref, stack) = refs[:-3], refs[-3:]
    if given:
        left_ref[...] = given[0][...]
        right_ref[...] = given[1][...]
    else:
        left_ref[...] = jnp.zeros_like(left_ref)
        right_ref[...] = jnp.zeros_like(right_ref)
    add_gram(rows, blocks, left_ref, right_ref, stack)


def gram(rows, blocks, given):
    width = blocks[0].shape[1]
    half = width // 2
    return pl.pallas_call(
        functools.partial(gram_kernel, len(blocks), rows),
        out_shape=[
            near((half, half)),
            near((width, half)),
        ],
        in_specs=[VMEM] * (len(blocks) + len(given)),
        out_specs=[VMEM] * 2,
        scratch_shapes=[pltpu.VMEM((len(blocks) * rows, width), jnp.float32)],
        cost_estimate=cost(0.4 * len(blocks)),
        compiler_params=grant(16),
        name="gram",
    )(*hold(*blocks, *given))


def solve_kernel(sizes, *refs):
    chips, rows, per_device, groups, total_rows, scale = sizes
    refs = list(refs)
    damping_ref, left_ref, right_ref = refs[:3]
    arrived = refs[3 : 3 + chips]
    passed = refs[3 + chips : 3 + 2 * chips]
    scores = refs[3 + 2 * chips : 3 + 3 * chips]
    left, right, stack, state, high, low, asked = refs[3 + 3 * chips :]
    half = left_ref.shape[0]
    width = 2 * half
    index = lax.axis_index("dp")
    chip, core = index // CORES, index % CORES
    pair = CORES * per_device
    total_queries = chips * pair
    group = total_queries // groups
    group_here = lax.axis_index("mod")

    for offset in range(chips):
        mine = arrived[offset][rows : rows + per_device]
        other = passed[offset][rows : rows + per_device]
        both = jnp.where(
            core == 0, jnp.concatenate([mine, other], 0), jnp.concatenate([other, mine], 0)
        )
        source = lax.bitwise_xor(chip, jnp.int32(offset))
        asked[pl.ds(pl.multiple_of(source * pair, pair), pair)] = both

    left[...] = left_ref[...]
    right[...] = right_ref[...]
    add_gram(rows, passed[1:], left, right, stack)

    diagonal = lax.broadcasted_iota(jnp.int32, (half, half), 0) == lax.broadcasted_iota(
        jnp.int32, (half, half), 1
    )
    eye = diagonal.astype(jnp.float32)
    first, cross, last = left[...], right[0:half], right[half:]
    trace = jnp.sum((first + last) * eye, keepdims=True).reshape(1, 1) / total_rows
    shift = damping_ref[chip] * trace / width
    first = first / total_rows + shift * eye
    last = last / total_rows + shift * eye
    cross = cross / total_rows
    squares = first * first + last * last + 2.0 * (cross * cross)
    inverse_norm = lax.rsqrt(jnp.sum(squares, keepdims=True).reshape(1, 1) + epsilon)
    cross = cross * inverse_norm
    state[0:half, 0:half] = first * inverse_norm
    state[0:half, half:] = cross
    state[half:width, 0:half] = cross.T
    state[half:width, half:] = last * inverse_norm
    for offset in range(groups):
        source = lax.bitwise_xor(group_here, jnp.int32(offset))
        state[width + offset * group : width + (offset + 1) * group] = (
            asked[pl.ds(pl.multiple_of(source * group, group), group)] * inverse_norm
        )

    for _ in range(NEWTON_STEPS - 1):
        high[...], low[...] = halves(state[...])

        def part(start, stop, column):
            columns = slice(column, column + half)
            return product_3(
                high[start:stop],
                low[start:stop],
                high[0:width, columns],
                low[0:width, columns],
            )

        state[0:half, 0:half] = 2.0 * state[0:half, 0:half] - part(0, half, 0)
        new = 2.0 * state[0:width, half:] - part(0, width, half)
        state[0:width, half:] = new
        state[half:width, 0:half] = new[0:half].T
        state[width:, 0:half] = 2.0 * state[width:, 0:half] - part(width, width + total_queries, 0)
        state[width:, half:] = 2.0 * state[width:, half:] - part(width, width + total_queries, half)

    high[...], low[...] = halves(state[...])
    conditioned = 2.0 * state[width:] - product_3(
        high[width:], low[width:], high[0:width], low[0:width]
    )
    conditioned_high, conditioned_low = halves(conditioned * scale)
    for offset in range(chips):
        block_high, block_low = halves(arrived[offset][0:rows])
        scores[offset][...] = product_3(
            conditioned_high, conditioned_low, block_high, block_low, (((1,), (1,)), ((), ()))
        )


def solve(sizes, damping, given, arrived, passed):
    chips, rows, per_device = sizes[:3]
    width = arrived[0].shape[1]
    half = width // 2
    total_queries = chips * CORES * per_device
    return pl.pallas_call(
        functools.partial(solve_kernel, sizes),
        out_shape=[near((total_queries, rows))] * chips,
        in_specs=[SMEM] + [VMEM] * (2 + 2 * chips),
        out_specs=[VMEM] * chips,
        scratch_shapes=[
            pltpu.VMEM((half, half), jnp.float32),
            pltpu.VMEM((width, half), jnp.float32),
            pltpu.VMEM(((chips - 1) * rows, width), jnp.float32),
            pltpu.VMEM((width + total_queries, width), jnp.float32),
            pltpu.VMEM((width + total_queries, width), jnp.bfloat16),
            pltpu.VMEM((width + total_queries, width), jnp.bfloat16),
            pltpu.VMEM((total_queries, width), jnp.float32),
        ],
        cost_estimate=cost(9.0),
        compiler_params=grant(24),
        name="solve",
    )(damping, *hold(*given, *arrived, *passed))


def swap(value, axis, offset):
    return lax.ppermute(value, axis, [(i, i ^ offset) for i in range(lax.axis_size(axis))])


def per_device(train_grads, queries, damping):
    rows, modules, width = train_grads.shape
    asked = queries.shape[0]
    devices = lax.axis_size("dp")
    groups = lax.axis_size("mod")
    chips = devices // CORES
    far = list(range(chips - 1, 0, -1))
    arrived = [None] * chips
    passed = [None] * chips
    packed = [None] * chips
    for offset in far + [0]:
        (packed[offset],) = pack((offset,), train_grads, queries)
    arrived[0] = packed[0]
    for offset in far:
        arrived[offset] = swap(packed[offset], "dp", offset * CORES)
    for offset in [0] + far:
        passed[offset] = swap(arrived[offset], "dp", 1)
    given = gram(rows, [arrived[0], passed[0]], ())
    given = gram(rows, [arrived[offset] for offset in far], given)
    sizes = (
        chips,
        rows,
        asked,
        groups,
        rows * devices,
        1.0 / math.sqrt(modules * groups * width),
    )
    scores = solve(sizes, damping, given, arrived, passed)
    total = scores[0]
    for offset in far:
        total = total + swap(scores[offset], "dp", offset * CORES)
    bit = groups // 2
    while bit:
        keep = total.shape[0] // 2
        total = total[:keep] + swap(total[keep:], "mod", bit)
        bit //= 2
    return total.T


def solution(mesh):
    return jax.shard_map(
        per_device,
        mesh=mesh,
        in_specs=(P("dp", "mod", None), P("dp", "mod", None), P("mod")),
        out_specs=P("dp", "mod"),
        check_vma=False,
    )
```

```python
import functools
import math

import jax
import jax.numpy as jnp
from jax import lax
from jax.experimental import pallas as pl
from jax.experimental.pallas import tpu as pltpu
from jax.sharding import PartitionSpec as P

NEWTON_STEPS = 8
CORES = 2
SOLVER = 1
PIECES = 4

epsilon = 1e-06

VMEM = pl.BlockSpec(memory_space=pltpu.VMEM)
SMEM = pl.BlockSpec(memory_space=pltpu.SMEM)
HBM = pl.BlockSpec(memory_space=pltpu.HBM)


def near(shape):
    return pltpu.VMEM(shape, jnp.float32)


def hold(*values):
    return [pltpu.with_memory_space_constraint(value, pltpu.VMEM) for value in values]


def grant(mebibytes):
    return pltpu.CompilerParams(vmem_limit_bytes=mebibytes << 20)


def cost(microseconds):
    return pl.CostEstimate(flops=int(microseconds * 1e9), bytes_accessed=0, transcendentals=0)


def halves(value):
    high = value.astype(jnp.bfloat16)
    return high, (value - high.astype(jnp.float32)).astype(jnp.bfloat16)


def product(left, right, dims=(((1,), (0,)), ((), ()))):
    return lax.dot_general(left, right, dims, preferred_element_type=jnp.float32)


def product_3(left_high, left_low, right_high, right_low, dims=(((1,), (0,)), ((), ()))):
    return (
        product(left_high, right_high, dims)
        + product(left_high, right_low, dims)
        + product(left_low, right_high, dims)
    )


def pack_kernel(rows_ref, queries_ref, *refs):
    rows, queries, row_sems, query_sem = refs[-4:]
    blocks = refs[:-4]
    chip = lax.axis_index("dp") // CORES
    total = rows_ref.shape[0]
    step = total // PIECES
    query_copy = pltpu.make_async_copy(queries_ref, queries, query_sem)
    copies = [
        pltpu.make_async_copy(
            rows_ref.at[pl.ds(piece * step, step)],
            rows.at[pl.ds(piece * step, step)],
            row_sems.at[piece],
        )
        for piece in range(PIECES)
    ]
    for copy in copies:
        copy.start()
    query_copy.start()
    modules = [lax.bitwise_xor(chip, jnp.int32(offset)) for offset in range(len(blocks))]
    for piece, copy in enumerate(copies):
        copy.wait()
        here = slice(piece * step, (piece + 1) * step)
        for module, block in zip(modules, blocks):
            block[here] = rows[here, module, :]
    query_copy.wait()
    for module, block in zip(modules, blocks):
        block[total:] = queries[:, module, :]


def pack(train_grads, queries):
    rows, modules, width = train_grads.shape
    return pl.pallas_call(
        pack_kernel,
        out_shape=[near((rows + queries.shape[0], width))] * modules,
        in_specs=[HBM, HBM],
        out_specs=[VMEM] * modules,
        scratch_shapes=[
            pltpu.VMEM(train_grads.shape, jnp.float32),
            pltpu.VMEM(queries.shape, jnp.float32),
            pltpu.SemaphoreType.DMA((PIECES,)),
            pltpu.SemaphoreType.DMA,
        ],
        compiler_params=grant(16),
        cost_estimate=cost(1.5),
        name="pack",
    )(*(pltpu.with_memory_space_constraint(value, pltpu.HBM) for value in (train_grads, queries)))


def add_gram(rows, blocks, left_ref, right_ref, stack):
    half = left_ref.shape[0]
    for place, block in enumerate(blocks):
        stack[place * rows : (place + 1) * rows] = block[0:rows]
    high, low = halves(stack[...])
    dims = (((0,), (0,)), ((), ()))
    left_ref[...] += product_3(high[:, :half], low[:, :half], high[:, :half], low[:, :half], dims)
    right_ref[...] += product_3(high, low, high[:, half:], low[:, half:], dims)


def first_gram_kernel(rows, damping_ref, one, two, left_ref, right_ref, damp_ref, stack):
    chip = lax.axis_index("dp") // CORES
    damp_ref[...] = jnp.full(damp_ref.shape, damping_ref[chip], jnp.float32)
    left_ref[...] = jnp.zeros_like(left_ref)
    right_ref[...] = jnp.zeros_like(right_ref)
    add_gram(rows, (one, two), left_ref, right_ref, stack)


def gram_kernel(rows, one, two, given_left, given_right, left_ref, right_ref, stack):
    left_ref[...] = given_left[...]
    right_ref[...] = given_right[...]
    add_gram(rows, (one, two), left_ref, right_ref, stack)


def gram(rows, pair, given=(), damping=None):
    width = pair[0].shape[1]
    half = width // 2
    shapes = [near((half, half)), near((width, half))]
    first = damping is not None
    return pl.pallas_call(
        functools.partial(first_gram_kernel if first else gram_kernel, rows),
        out_shape=shapes + [near((8, 128))] * first,
        in_specs=[SMEM] * first + [VMEM] * (2 + len(given)),
        out_specs=[VMEM] * (2 + first),
        scratch_shapes=[pltpu.VMEM((2 * rows, width), jnp.float32)],
        compiler_params=grant(16),
        cost_estimate=cost(0.6),
        name="gram",
    )(*([damping] * first), *hold(*pair, *given))


def solve_kernel(sizes, *refs):
    chips, rows, per_device, groups, total_rows, scale = sizes
    refs = list(refs)
    damp_ref, left_ref, right_ref = refs[:3]
    blocks = [refs[3 + CORES * offset : 3 + CORES * (offset + 1)] for offset in range(chips)]
    scores = refs[3 + CORES * chips : 3 + (CORES + 1) * chips]
    left, right, stack, state, high, low, asked = refs[3 + (CORES + 1) * chips :]
    half = left_ref.shape[0]
    width = 2 * half
    chip = lax.axis_index("dp") // CORES
    pair = CORES * per_device
    total_queries = chips * pair
    group = total_queries // groups
    group_here = lax.axis_index("mod")

    for offset in range(chips):
        source = lax.bitwise_xor(chip, jnp.int32(offset))
        asked[pl.ds(pl.multiple_of(source * pair, pair), pair)] = jnp.concatenate(
            [block[rows : rows + per_device] for block in blocks[offset]], 0
        )

    left[...] = left_ref[...]
    right[...] = right_ref[...]
    add_gram(rows, blocks[-1], left, right, stack)

    diagonal = lax.broadcasted_iota(jnp.int32, (half, half), 0) == lax.broadcasted_iota(
        jnp.int32, (half, half), 1
    )
    eye = diagonal.astype(jnp.float32)
    first, cross, last = left[...], right[0:half], right[half:]
    trace = jnp.sum((first + last) * eye, keepdims=True).reshape(1, 1) / total_rows
    shift = damp_ref[0:1, 0:1] * trace / width
    first = first / total_rows + shift * eye
    last = last / total_rows + shift * eye
    cross = cross / total_rows
    squares = first * first + last * last + 2.0 * (cross * cross)
    inverse_norm = lax.rsqrt(jnp.sum(squares, keepdims=True).reshape(1, 1) + epsilon)
    cross = cross * inverse_norm
    state[0:half, 0:half] = first * inverse_norm
    state[0:half, half:] = cross
    state[half:width, 0:half] = cross.T
    state[half:width, half:] = last * inverse_norm
    for offset in range(groups):
        source = lax.bitwise_xor(group_here, jnp.int32(offset))
        state[width + offset * group : width + (offset + 1) * group] = (
            asked[pl.ds(pl.multiple_of(source * group, group), group)] * inverse_norm
        )

    for _ in range(NEWTON_STEPS - 1):
        high[...], low[...] = halves(state[...])

        def part(start, stop, column):
            columns = slice(column, column + half)
            return product_3(
                high[start:stop],
                low[start:stop],
                high[0:width, columns],
                low[0:width, columns],
            )

        state[0:half, 0:half] = 2.0 * state[0:half, 0:half] - part(0, half, 0)
        new = 2.0 * state[0:width, half:] - part(0, width, half)
        state[0:width, half:] = new
        state[half:width, 0:half] = new[0:half].T
        state[width:, 0:half] = 2.0 * state[width:, 0:half] - part(width, width + total_queries, 0)
        state[width:, half:] = 2.0 * state[width:, half:] - part(width, width + total_queries, half)

    high[...], low[...] = halves(state[...])
    conditioned = 2.0 * state[width:] - product_3(
        high[width:], low[width:], high[0:width], low[0:width]
    )
    conditioned_high, conditioned_low = halves(conditioned * scale)
    for offset in range(chips):
        for place, block in enumerate(blocks[offset]):
            block_high, block_low = halves(block[0:rows])
            scores[offset][:, place * rows : (place + 1) * rows] = product_3(
                conditioned_high, conditioned_low, block_high, block_low, (((1,), (1,)), ((), ()))
            )


def solve(sizes, damp, given, blocks):
    chips, rows, per_device = sizes[:3]
    width = blocks[0].shape[1]
    half = width // 2
    total_queries = chips * CORES * per_device
    return pl.pallas_call(
        functools.partial(solve_kernel, sizes),
        out_shape=[near((total_queries, CORES * rows))] * chips,
        in_specs=[VMEM] * (3 + CORES * chips),
        out_specs=[VMEM] * chips,
        scratch_shapes=[
            pltpu.VMEM((half, half), jnp.float32),
            pltpu.VMEM((width, half), jnp.float32),
            pltpu.VMEM((CORES * rows, width), jnp.float32),
            pltpu.VMEM((width + total_queries, width), jnp.float32),
            pltpu.VMEM((width + total_queries, width), jnp.bfloat16),
            pltpu.VMEM((width + total_queries, width), jnp.bfloat16),
            pltpu.VMEM((total_queries, width), jnp.float32),
        ],
        compiler_params=grant(24),
        cost_estimate=cost(9.0),
        name="solve",
    )(*hold(damp, *given, *blocks))


def send(value, axis, offset, source=SOLVER, target=SOLVER):
    chips = lax.axis_size("dp") // CORES
    pairs = [
        (CORES * chip + source, CORES * (chip ^ offset) + target) for chip in range(chips)
    ]
    return lax.ppermute(value, axis, pairs)


def swap(value, offset):
    devices, groups = lax.axis_size("dp"), lax.axis_size("mod")
    pairs = [
        (group * devices + device, (group ^ offset) * devices + device)
        for group in range(groups)
        for device in range(SOLVER, devices, CORES)
    ]
    return lax.ppermute(value, ("mod", "dp"), pairs)


def per_device(train_grads, queries, damping):
    rows, modules, width = train_grads.shape
    devices = lax.axis_size("dp")
    groups = lax.axis_size("mod")
    chips = devices // CORES
    packed = pack(train_grads, queries)
    blocks = [[None] * CORES for _ in range(chips)]
    for offset in range(chips):
        for core in range(CORES):
            blocks[offset][core] = (
                packed[0]
                if (offset, core) == (0, SOLVER)
                else send(packed[offset], "dp", offset, source=core)
            )
    *given, damp = gram(rows, blocks[0], damping=damping)
    for offset in range(1, chips - 1):
        given = gram(rows, blocks[offset], given)
    sizes = (
        chips,
        rows,
        queries.shape[0],
        groups,
        rows * devices,
        1.0 / math.sqrt(modules * groups * width),
    )
    scores = solve(sizes, damp, given, sum(blocks, []))
    total = scores[0]
    for offset in range(chips - 1, 0, -1):
        total = total + send(scores[offset], "dp", offset)
    bit = groups // 2
    while bit:
        keep = total.shape[0] // 2
        total = total[:keep] + swap(total[keep:], bit)
        bit //= 2
    own = lax.axis_index("dp") % CORES == SOLVER
    result = jnp.where(
        own, total[:, SOLVER * rows :], send(total[:, :rows], "dp", 0, target=1 - SOLVER)
    )
    return result.T


def solution(mesh):
    return jax.shard_map(
        per_device,
        mesh=mesh,
        in_specs=(P("dp", "mod", None), P("dp", "mod", None), P("mod")),
        out_specs=P("dp", "mod"),
        check_vma=False,
    )
```

```python
import functools
import math

import jax
import jax.numpy as jnp
from jax import lax
from jax.experimental import pallas as pl
from jax.experimental.pallas import tpu as pltpu
from jax.sharding import PartitionSpec as P

NEWTON_STEPS = 8
CORES = 2
SOLVER = 1
PIECES = 4

epsilon = 1e-06

VMEM = pl.BlockSpec(memory_space=pltpu.VMEM)
SMEM = pl.BlockSpec(memory_space=pltpu.SMEM)
HBM = pl.BlockSpec(memory_space=pltpu.HBM)


def near(shape):
    return pltpu.VMEM(shape, jnp.float32)


def hold(*values):
    return [pltpu.with_memory_space_constraint(value, pltpu.VMEM) for value in values]


def grant(mebibytes):
    return pltpu.CompilerParams(vmem_limit_bytes=mebibytes << 20)


def cost(microseconds):
    return pl.CostEstimate(flops=int(microseconds * 1e9), bytes_accessed=0, transcendentals=0)


def halves(value):
    high = value.astype(jnp.bfloat16)
    return high, (value - high.astype(jnp.float32)).astype(jnp.bfloat16)


def product(left, right, dims=(((1,), (0,)), ((), ()))):
    return lax.dot_general(left, right, dims, preferred_element_type=jnp.float32)


def product_3(left_high, left_low, right_high, right_low, dims=(((1,), (0,)), ((), ()))):
    return (
        product(left_high, right_high, dims)
        + product(left_high, right_low, dims)
        + product(left_low, right_high, dims)
    )


def pack_kernel(rows_ref, queries_ref, *refs):
    rows, queries, row_sems, query_sem = refs[-4:]
    blocks = refs[:-4]
    chip = lax.axis_index("dp") // CORES
    total = rows_ref.shape[0]
    step = total // PIECES
    query_copy = pltpu.make_async_copy(queries_ref, queries, query_sem)
    copies = [
        pltpu.make_async_copy(
            rows_ref.at[pl.ds(piece * step, step)],
            rows.at[pl.ds(piece * step, step)],
            row_sems.at[piece],
        )
        for piece in range(PIECES)
    ]
    for copy in copies:
        copy.start()
    query_copy.start()
    modules = [lax.bitwise_xor(chip, jnp.int32(offset)) for offset in range(len(blocks))]
    for piece, copy in enumerate(copies):
        copy.wait()
        here = slice(piece * step, (piece + 1) * step)
        for module, block in zip(modules, blocks):
            block[here] = rows[here, module, :]
    query_copy.wait()
    for module, block in zip(modules, blocks):
        block[total:] = queries[:, module, :]


def pack(train_grads, queries):
    rows, modules, width = train_grads.shape
    return pl.pallas_call(
        pack_kernel,
        out_shape=[near((rows + queries.shape[0], width))] * modules,
        in_specs=[HBM, HBM],
        out_specs=[VMEM] * modules,
        scratch_shapes=[
            pltpu.VMEM(train_grads.shape, jnp.float32),
            pltpu.VMEM(queries.shape, jnp.float32),
            pltpu.SemaphoreType.DMA((PIECES,)),
            pltpu.SemaphoreType.DMA,
        ],
        compiler_params=grant(16),
        cost_estimate=cost(1.5),
        name="pack",
    )(*(pltpu.with_memory_space_constraint(value, pltpu.HBM) for value in (train_grads, queries)))


def add_gram(rows, blocks, left_ref, right_ref, stack):
    half = left_ref.shape[0]
    for place, block in enumerate(blocks):
        stack[place * rows : (place + 1) * rows] = block[0:rows]
    high, low = halves(stack[...])
    dims = (((0,), (0,)), ((), ()))
    left_ref[...] += product_3(high[:, :half], low[:, :half], high[:, :half], low[:, :half], dims)
    right_ref[...] += product_3(high, low, high[:, half:], low[:, half:], dims)


def on_solver(body):
    pl.when(lax.axis_index("dp") % CORES == SOLVER)(body)


def first_gram_kernel(rows, damping_ref, one, two, left_ref, right_ref, damp_ref, stack):
    chip = lax.axis_index("dp") // CORES
    damp_ref[...] = jnp.full(damp_ref.shape, damping_ref[chip], jnp.float32)

    @on_solver
    def _():
        left_ref[...] = jnp.zeros_like(left_ref)
        right_ref[...] = jnp.zeros_like(right_ref)
        add_gram(rows, (one, two), left_ref, right_ref, stack)


def gram_kernel(rows, one, two, given_left, given_right, left_ref, right_ref, stack):
    @on_solver
    def _():
        left_ref[...] = given_left[...]
        right_ref[...] = given_right[...]
        add_gram(rows, (one, two), left_ref, right_ref, stack)


def gram(rows, pair, given=(), damping=None):
    width = pair[0].shape[1]
    half = width // 2
    shapes = [near((half, half)), near((width, half))]
    first = damping is not None
    return pl.pallas_call(
        functools.partial(first_gram_kernel if first else gram_kernel, rows),
        out_shape=shapes + [near((8, 128))] * first,
        in_specs=[SMEM] * first + [VMEM] * (2 + len(given)),
        out_specs=[VMEM] * (2 + first),
        scratch_shapes=[pltpu.VMEM((2 * rows, width), jnp.float32)],
        compiler_params=grant(16),
        cost_estimate=cost(0.6),
        name="gram",
    )(*([damping] * first), *hold(*pair, *given))


def solve_kernel(sizes, *refs):
    chips = sizes[0]
    scores = refs[3 + CORES * chips : 3 + (CORES + 1) * chips]

    @pl.when(lax.axis_index("dp") % CORES != SOLVER)
    def _():
        for score in scores:
            score[...] = jnp.zeros_like(score)

    on_solver(functools.partial(solve_module, sizes, *refs))


def solve_module(sizes, *refs):
    chips, rows, per_device, groups, total_rows, scale = sizes
    refs = list(refs)
    damp_ref, left_ref, right_ref = refs[:3]
    blocks = [refs[3 + CORES * offset : 3 + CORES * (offset + 1)] for offset in range(chips)]
    scores = refs[3 + CORES * chips : 3 + (CORES + 1) * chips]
    left, right, stack, state, high, low, asked = refs[3 + (CORES + 1) * chips :]
    half = left_ref.shape[0]
    width = 2 * half
    chip = lax.axis_index("dp") // CORES
    pair = CORES * per_device
    total_queries = chips * pair
    group = total_queries // groups
    group_here = lax.axis_index("mod")

    for offset in range(chips):
        source = lax.bitwise_xor(chip, jnp.int32(offset))
        asked[pl.ds(pl.multiple_of(source * pair, pair), pair)] = jnp.concatenate(
            [block[rows : rows + per_device] for block in blocks[offset]], 0
        )

    left[...] = left_ref[...]
    right[...] = right_ref[...]
    add_gram(rows, blocks[-1], left, right, stack)

    diagonal = lax.broadcasted_iota(jnp.int32, (half, half), 0) == lax.broadcasted_iota(
        jnp.int32, (half, half), 1
    )
    eye = diagonal.astype(jnp.float32)
    first, cross, last = left[...], right[0:half], right[half:]
    trace = jnp.sum((first + last) * eye, keepdims=True).reshape(1, 1) / total_rows
    shift = damp_ref[0:1, 0:1] * trace / width
    first = first / total_rows + shift * eye
    last = last / total_rows + shift * eye
    cross = cross / total_rows
    squares = first * first + last * last + 2.0 * (cross * cross)
    inverse_norm = lax.rsqrt(jnp.sum(squares, keepdims=True).reshape(1, 1) + epsilon)
    cross = cross * inverse_norm
    state[0:half, 0:half] = first * inverse_norm
    state[0:half, half:] = cross
    state[half:width, 0:half] = cross.T
    state[half:width, half:] = last * inverse_norm
    for offset in range(groups):
        source = lax.bitwise_xor(group_here, jnp.int32(offset))
        state[width + offset * group : width + (offset + 1) * group] = (
            asked[pl.ds(pl.multiple_of(source * group, group), group)] * inverse_norm
        )

    for _ in range(NEWTON_STEPS - 1):
        high[...], low[...] = halves(state[...])

        def part(start, stop, column):
            columns = slice(column, column + half)
            return product_3(
                high[start:stop],
                low[start:stop],
                high[0:width, columns],
                low[0:width, columns],
            )

        state[0:half, 0:half] = 2.0 * state[0:half, 0:half] - part(0, half, 0)
        new = 2.0 * state[0:width, half:] - part(0, width, half)
        state[0:width, half:] = new
        state[half:width, 0:half] = new[0:half].T
        state[width:, 0:half] = 2.0 * state[width:, 0:half] - part(width, width + total_queries, 0)
        state[width:, half:] = 2.0 * state[width:, half:] - part(width, width + total_queries, half)

    high[...], low[...] = halves(state[...])
    conditioned = 2.0 * state[width:] - product_3(
        high[width:], low[width:], high[0:width], low[0:width]
    )
    conditioned_high, conditioned_low = halves(conditioned * scale)
    for offset in range(chips):
        for place, block in enumerate(blocks[offset]):
            block_high, block_low = halves(block[0:rows])
            scores[offset][:, place * rows : (place + 1) * rows] = product_3(
                conditioned_high, conditioned_low, block_high, block_low, (((1,), (1,)), ((), ()))
            )


def solve(sizes, damp, given, blocks):
    chips, rows, per_device = sizes[:3]
    width = blocks[0].shape[1]
    half = width // 2
    total_queries = chips * CORES * per_device
    return pl.pallas_call(
        functools.partial(solve_kernel, sizes),
        out_shape=[near((total_queries, CORES * rows))] * chips,
        in_specs=[VMEM] * (3 + CORES * chips),
        out_specs=[VMEM] * chips,
        scratch_shapes=[
            pltpu.VMEM((half, half), jnp.float32),
            pltpu.VMEM((width, half), jnp.float32),
            pltpu.VMEM((CORES * rows, width), jnp.float32),
            pltpu.VMEM((width + total_queries, width), jnp.float32),
            pltpu.VMEM((width + total_queries, width), jnp.bfloat16),
            pltpu.VMEM((width + total_queries, width), jnp.bfloat16),
            pltpu.VMEM((total_queries, width), jnp.float32),
        ],
        compiler_params=grant(24),
        cost_estimate=cost(9.0),
        name="solve",
    )(*hold(damp, *given, *blocks))


def swap(value, axis, offset):
    return lax.ppermute(value, axis, [(i, i ^ offset) for i in range(lax.axis_size(axis))])


def per_device(train_grads, queries, damping):
    rows, modules, width = train_grads.shape
    devices = lax.axis_size("dp")
    groups = lax.axis_size("mod")
    chips = devices // CORES
    packed = pack(train_grads, queries)
    arrived = [packed[0]]
    for offset in range(1, chips):
        arrived.append(swap(packed[offset], "dp", CORES * offset))
    blocks = [[swap(block, "dp", 1), block] for block in arrived]
    *given, damp = gram(rows, blocks[0], damping=damping)
    for offset in range(1, chips - 1):
        given = gram(rows, blocks[offset], given)
    sizes = (
        chips,
        rows,
        queries.shape[0],
        groups,
        rows * devices,
        1.0 / math.sqrt(modules * groups * width),
    )
    scores = solve(sizes, damp, given, sum(blocks, []))
    total = scores[0]
    for offset in range(chips - 1, 0, -1):
        total = total + swap(scores[offset], "dp", CORES * offset)
    bit = groups // 2
    while bit:
        keep = total.shape[0] // 2
        total = total[:keep] + swap(total[keep:], "mod", bit)
        bit //= 2
    solver = lax.axis_index("dp") % CORES == SOLVER
    result = jnp.where(solver, total[:, SOLVER * rows :], swap(total[:, :rows], "dp", 1))
    return result.T


def solution(mesh):
    return jax.shard_map(
        per_device,
        mesh=mesh,
        in_specs=(P("dp", "mod", None), P("dp", "mod", None), P("mod")),
        out_specs=P("dp", "mod"),
        check_vma=False,
    )
```

```python
import functools
import math

import jax
import jax.numpy as jnp
from jax import lax
from jax.experimental import pallas as pl
from jax.experimental.pallas import tpu as pltpu
from jax.sharding import PartitionSpec as P


NEWTON_STEPS = 8
SQUARINGS = 6
CORES = 2
SOLVER = 1
PIECES = 4

epsilon = 1e-06

VMEM = pl.BlockSpec(memory_space=pltpu.VMEM)
SMEM = pl.BlockSpec(memory_space=pltpu.SMEM)
HBM = pl.BlockSpec(memory_space=pltpu.HBM)


def near(shape):
    return pltpu.VMEM(shape, jnp.float32)


def hold(*values):
    return [pltpu.with_memory_space_constraint(value, pltpu.VMEM) for value in values]


def grant(mebibytes):
    return pltpu.CompilerParams(vmem_limit_bytes=mebibytes << 20)


def cost(microseconds):
    return pl.CostEstimate(flops=int(microseconds * 1e9), bytes_accessed=0, transcendentals=0)


def halves(value):
    high = value.astype(jnp.bfloat16)
    return high, (value - high.astype(jnp.float32)).astype(jnp.bfloat16)


def product(left, right, dims=(((1,), (0,)), ((), ()))):
    return lax.dot_general(left, right, dims, preferred_element_type=jnp.float32)


def product_3(left_high, left_low, right_high, right_low, dims=(((1,), (0,)), ((), ()))):
    return (
        product(left_high, right_high, dims)
        + product(left_high, right_low, dims)
        + product(left_low, right_high, dims)
    )


def narrow_product(left, right_high, right_low, dims=(((1,), (0,)), ((), ()))):
    high, low = halves(left)
    count = left.shape[0]
    both = product(jnp.concatenate([high, low], 0), right_high, dims)
    return both[:count] + both[count:] + product(high, right_low, dims)


def pack_kernel(rows_ref, queries_ref, *refs):
    rows, queries, row_sems, query_sem = refs[-4:]
    blocks = refs[:-4]
    chip = lax.axis_index("dp") // CORES
    total = rows_ref.shape[0]
    step = total // PIECES
    query_copy = pltpu.make_async_copy(queries_ref, queries, query_sem)
    copies = [
        pltpu.make_async_copy(
            rows_ref.at[pl.ds(piece * step, step)],
            rows.at[pl.ds(piece * step, step)],
            row_sems.at[piece],
        )
        for piece in range(PIECES)
    ]
    for copy in copies:
        copy.start()
    query_copy.start()
    modules = [lax.bitwise_xor(chip, jnp.int32(offset)) for offset in range(len(blocks))]
    for piece, copy in enumerate(copies):
        copy.wait()
        here = slice(piece * step, (piece + 1) * step)
        for module, block in zip(modules, blocks):
            block[here] = rows[here, module, :]
    query_copy.wait()
    for module, block in zip(modules, blocks):
        block[total:] = queries[:, module, :]


def pack(train_grads, queries):
    rows, modules, width = train_grads.shape
    return pl.pallas_call(
        pack_kernel,
        out_shape=[near((rows + queries.shape[0], width))] * modules,
        in_specs=[HBM, HBM],
        out_specs=[VMEM] * modules,
        scratch_shapes=[
            pltpu.VMEM(train_grads.shape, jnp.float32),
            pltpu.VMEM(queries.shape, jnp.float32),
            pltpu.SemaphoreType.DMA((PIECES,)),
            pltpu.SemaphoreType.DMA,
        ],
        compiler_params=grant(16),
        cost_estimate=cost(1.5),
        name="pack",
    )(*(pltpu.with_memory_space_constraint(value, pltpu.HBM) for value in (train_grads, queries)))


def add_gram(rows, blocks, left_ref, right_ref, stack):
    half = left_ref.shape[0]
    for place, block in enumerate(blocks):
        stack[place * rows : (place + 1) * rows] = block[0:rows]
    high, low = halves(stack[...])
    dims = (((0,), (0,)), ((), ()))
    left_ref[...] += product_3(high[:, :half], low[:, :half], high[:, :half], low[:, :half], dims)
    right_ref[...] += product_3(high, low, high[:, half:], low[:, half:], dims)


def on_solver(body):
    pl.when(lax.axis_index("dp") % CORES == SOLVER)(body)


def first_gram_kernel(rows, damping_ref, one, two, left_ref, right_ref, damp_ref, stack):
    chip = lax.axis_index("dp") // CORES
    damp_ref[...] = jnp.full(damp_ref.shape, damping_ref[chip], jnp.float32)

    @on_solver
    def _():
        left_ref[...] = jnp.zeros_like(left_ref)
        right_ref[...] = jnp.zeros_like(right_ref)
        add_gram(rows, (one, two), left_ref, right_ref, stack)


def gram_kernel(rows, one, two, given_left, given_right, left_ref, right_ref, stack):
    @on_solver
    def _():
        left_ref[...] = given_left[...]
        right_ref[...] = given_right[...]
        add_gram(rows, (one, two), left_ref, right_ref, stack)


def gram(rows, pair, given=(), damping=None):
    width = pair[0].shape[1]
    half = width // 2
    shapes = [near((half, half)), near((width, half))]
    first = damping is not None
    return pl.pallas_call(
        functools.partial(first_gram_kernel if first else gram_kernel, rows),
        out_shape=shapes + [near((8, 128))] * first,
        in_specs=[SMEM] * first + [VMEM] * (2 + len(given)),
        out_specs=[VMEM] * (2 + first),
        scratch_shapes=[pltpu.VMEM((2 * rows, width), jnp.float32)],
        compiler_params=grant(16),
        cost_estimate=cost(0.6),
        name="gram",
    )(*([damping] * first), *hold(*pair, *given))


def solve_kernel(sizes, *refs):
    chips = sizes[0]
    scores = refs[3 + CORES * chips : 3 + (CORES + 1) * chips]

    @pl.when(lax.axis_index("dp") % CORES != SOLVER)
    def _():
        for score in scores:
            score[...] = jnp.zeros_like(score)

    on_solver(functools.partial(solve_module, sizes, *refs))


def solve_module(sizes, *refs):
    chips, rows, per_device, groups, total_rows, scale = sizes
    refs = list(refs)
    damp_ref, left_ref, right_ref = refs[:3]
    blocks = [refs[3 + CORES * offset : 3 + CORES * (offset + 1)] for offset in range(chips)]
    scores = refs[3 + CORES * chips : 3 + (CORES + 1) * chips]
    left, right, stack, state, high, low, asked = refs[3 + (CORES + 1) * chips :]
    half = left_ref.shape[0]
    width = 2 * half
    chip = lax.axis_index("dp") // CORES
    pair = CORES * per_device
    total_queries = chips * pair
    group = total_queries // groups
    group_here = lax.axis_index("mod")

    for offset in range(chips):
        source = lax.bitwise_xor(chip, jnp.int32(offset))
        asked[pl.ds(pl.multiple_of(source * pair, pair), pair)] = jnp.concatenate(
            [block[rows : rows + per_device] for block in blocks[offset]], 0
        )

    left[...] = left_ref[...]
    right[...] = right_ref[...]
    add_gram(rows, blocks[-1], left, right, stack)

    diagonal = lax.broadcasted_iota(jnp.int32, (half, half), 0) == lax.broadcasted_iota(
        jnp.int32, (half, half), 1
    )
    eye = diagonal.astype(jnp.float32)
    first, cross, last = left[...], right[0:half], right[half:]
    trace = jnp.sum((first + last) * eye, keepdims=True).reshape(1, 1) / total_rows
    shift = damp_ref[0:1, 0:1] * trace / width
    first = first / total_rows + shift * eye
    last = last / total_rows + shift * eye
    cross = cross / total_rows
    squares = first * first + last * last + 2.0 * (cross * cross)
    inverse_norm = lax.rsqrt(jnp.sum(squares, keepdims=True).reshape(1, 1) + epsilon)
    cross = cross * inverse_norm
    state[0:half, 0:half] = first * inverse_norm
    state[0:half, half:] = cross
    state[half:width, 0:half] = cross.T
    state[half:width, half:] = last * inverse_norm
    for offset in range(groups):
        source = lax.bitwise_xor(group_here, jnp.int32(offset))
        state[width + offset * group : width + (offset + 1) * group] = (
            asked[pl.ds(pl.multiple_of(source * group, group), group)] * inverse_norm
        )

    for _ in range(SQUARINGS):
        high[...], low[...] = halves(state[...])

        def part(start, stop, column):
            columns = slice(column, column + half)
            return product_3(
                high[start:stop],
                low[start:stop],
                high[0:width, columns],
                low[0:width, columns],
            )

        state[0:half, 0:half] = 2.0 * state[0:half, 0:half] - part(0, half, 0)
        new = 2.0 * state[0:width, half:] - part(0, width, half)
        state[0:width, half:] = new
        state[half:width, 0:half] = new[0:half].T
        state[width:, 0:half] = 2.0 * state[width:, 0:half] - part(width, width + total_queries, 0)
        state[width:, half:] = 2.0 * state[width:, half:] - part(width, width + total_queries, half)

    high[...], low[...] = halves(state[...])
    asked_last = state[width:]
    conditioned = asked_last
    for _ in range(2 ** (NEWTON_STEPS - SQUARINGS) - 1):
        moved = narrow_product(conditioned, high[0:width], low[0:width])
        conditioned = asked_last + (conditioned - moved)
    conditioned = conditioned * scale
    for offset in range(chips):
        for place, block in enumerate(blocks[offset]):
            stack[place * rows : (place + 1) * rows] = block[0:rows]
        rows_high, rows_low = halves(stack[...])
        scores[offset][...] = narrow_product(
            conditioned, rows_high, rows_low, (((1,), (1,)), ((), ()))
        )


def solve(sizes, damp, given, blocks):
    chips, rows, per_device = sizes[:3]
    width = blocks[0].shape[1]
    half = width // 2
    total_queries = chips * CORES * per_device
    return pl.pallas_call(
        functools.partial(solve_kernel, sizes),
        out_shape=[near((total_queries, CORES * rows))] * chips,
        in_specs=[VMEM] * (3 + CORES * chips),
        out_specs=[VMEM] * chips,
        scratch_shapes=[
            pltpu.VMEM((half, half), jnp.float32),
            pltpu.VMEM((width, half), jnp.float32),
            pltpu.VMEM((CORES * rows, width), jnp.float32),
            pltpu.VMEM((width + total_queries, width), jnp.float32),
            pltpu.VMEM((width + total_queries, width), jnp.bfloat16),
            pltpu.VMEM((width + total_queries, width), jnp.bfloat16),
            pltpu.VMEM((total_queries, width), jnp.float32),
        ],
        compiler_params=grant(24),
        cost_estimate=cost(9.0),
        name="solve",
    )(*hold(damp, *given, *blocks))


def swap(value, axis, offset):
    return lax.ppermute(value, axis, [(i, i ^ offset) for i in range(lax.axis_size(axis))])


def route(value, to_solver, others):
    devices, groups = lax.axis_size("dp"), lax.axis_size("mod")
    pairs = []
    for group in range(groups):
        for device in range(devices):
            goal = to_solver(group, device)
            if goal is None:
                goal = others(group, device)
            pairs.append((group * devices + device, goal[0] * devices + goal[1]))
    return lax.ppermute(value, ("mod", "dp"), pairs)


def same_core(value, offset):
    return route(
        value,
        lambda group, device: (group, device ^ (CORES * offset)) if device % CORES == SOLVER else None,
        lambda group, device: (group ^ 1, device),
    )


def cross_core(value, offset):
    return route(
        value,
        lambda group, device: None
        if device % CORES == SOLVER
        else (group, (device ^ (CORES * offset)) ^ 1),
        lambda group, device: (group, device ^ 1),
    )


def sequence(chips):
    steps = []
    for first in range(1, chips, 2):
        offsets = range(first, min(first + 2, chips))
        steps += [("same", offset) for offset in offsets]
        steps += [("cross", offset) for offset in offsets]
    return steps + [("cross", 0)]


def influence(train_grads, queries, damping):
    rows, modules, width = train_grads.shape
    devices = lax.axis_size("dp")
    groups = lax.axis_size("mod")
    chips = devices // CORES
    packed = pack(train_grads, queries)
    arrived = {("same", 0): packed[0]}
    for kind, offset in sequence(chips):
        mover = same_core if kind == "same" else cross_core
        arrived[kind, offset] = mover(packed[offset], offset)
    blocks = [[arrived["cross", offset], arrived["same", offset]] for offset in range(chips)]
    *given, damp = gram(rows, blocks[0], damping=damping)
    for offset in range(1, chips - 1):
        given = gram(rows, blocks[offset], given)
    sizes = (
        chips,
        rows,
        queries.shape[0],
        groups,
        rows * devices,
        1.0 / math.sqrt(modules * groups * width),
    )
    scores = solve(sizes, damp, given, sum(blocks, []))
    total = scores[0]
    for offset in range(chips - 1, 0, -1):
        total = total + swap(scores[offset], "dp", CORES * offset)
    bit = groups // 2
    while bit:
        keep = total.shape[0] // 2
        total = total[:keep] + swap(total[keep:], "mod", bit)
        bit //= 2
    solver = lax.axis_index("dp") % CORES == SOLVER
    result = jnp.where(solver, total[:, SOLVER * rows :], swap(total[:, :rows], "dp", 1))
    return result.T


def solution(mesh):
    return jax.shard_map(
        influence,
        mesh=mesh,
        in_specs=(P("dp", "mod", None), P("dp", "mod", None), P("mod")),
        out_specs=P("dp", "mod"),
        check_vma=False,
    )
```

```python
import functools
import math

import jax
import jax.numpy as jnp
from jax import lax
from jax.experimental import pallas as pl
from jax.experimental.pallas import tpu as pltpu
from jax.sharding import PartitionSpec as P


NEWTON_STEPS = 8
SQUARINGS = 6
CORES = 2
SOLVER = 1
PIECES = 4

epsilon = 1e-06

VMEM = pl.BlockSpec(memory_space=pltpu.VMEM)
SMEM = pl.BlockSpec(memory_space=pltpu.SMEM)
HBM = pl.BlockSpec(memory_space=pltpu.HBM)


def near(shape):
    return pltpu.VMEM(shape, jnp.float32)


def hold(*values):
    return [pltpu.with_memory_space_constraint(value, pltpu.VMEM) for value in values]


def grant(mebibytes):
    return pltpu.CompilerParams(vmem_limit_bytes=mebibytes << 20)


def cost(microseconds):
    return pl.CostEstimate(flops=int(microseconds * 1e9), bytes_accessed=0, transcendentals=0)


def halves(value):
    high = value.astype(jnp.bfloat16)
    return high, (value - high.astype(jnp.float32)).astype(jnp.bfloat16)


def product(left, right, dims=(((1,), (0,)), ((), ()))):
    return lax.dot_general(left, right, dims, preferred_element_type=jnp.float32)


def product_3(left_high, left_low, right_high, right_low, dims=(((1,), (0,)), ((), ()))):
    return (
        product(left_high, right_high, dims)
        + product(left_high, right_low, dims)
        + product(left_low, right_high, dims)
    )


def narrow_product(left, right_high, right_low, dims=(((1,), (0,)), ((), ()))):
    high, low = halves(left)
    count = left.shape[0]
    both = product(jnp.concatenate([high, low], 0), right_high, dims)
    return both[:count] + both[count:] + product(high, right_low, dims)


def pack_kernel(rows_ref, queries_ref, *refs):
    rows, queries, row_sems, query_sem = refs[-4:]
    blocks = refs[:-4]
    chip = lax.axis_index("dp") // CORES
    total = rows_ref.shape[0]
    step = total // PIECES
    query_copy = pltpu.make_async_copy(queries_ref, queries, query_sem)
    copies = [
        pltpu.make_async_copy(
            rows_ref.at[pl.ds(piece * step, step)],
            rows.at[pl.ds(piece * step, step)],
            row_sems.at[piece],
        )
        for piece in range(PIECES)
    ]
    for copy in copies:
        copy.start()
    query_copy.start()
    modules = [lax.bitwise_xor(chip, jnp.int32(offset)) for offset in range(len(blocks))]
    for piece, copy in enumerate(copies):
        copy.wait()
        here = slice(piece * step, (piece + 1) * step)
        for module, block in zip(modules, blocks):
            block[here] = rows[here, module, :]
    query_copy.wait()
    for module, block in zip(modules, blocks):
        block[total:] = queries[:, module, :]


def pack(train_grads, queries):
    rows, modules, width = train_grads.shape
    return pl.pallas_call(
        pack_kernel,
        out_shape=[near((rows + queries.shape[0], width))] * modules,
        in_specs=[HBM, HBM],
        out_specs=[VMEM] * modules,
        scratch_shapes=[
            pltpu.VMEM(train_grads.shape, jnp.float32),
            pltpu.VMEM(queries.shape, jnp.float32),
            pltpu.SemaphoreType.DMA((PIECES,)),
            pltpu.SemaphoreType.DMA,
        ],
        compiler_params=grant(16),
        cost_estimate=cost(1.5),
        name="pack",
    )(*(pltpu.with_memory_space_constraint(value, pltpu.HBM) for value in (train_grads, queries)))


def add_gram(rows, blocks, left_ref, right_ref, stack):
    half = left_ref.shape[0]
    for place, block in enumerate(blocks):
        stack[place * rows : (place + 1) * rows] = block[0:rows]
    high, low = halves(stack[...])
    dims = (((0,), (0,)), ((), ()))
    left_ref[...] += product_3(high[:, :half], low[:, :half], high[:, :half], low[:, :half], dims)
    right_ref[...] += product_3(high, low, high[:, half:], low[:, half:], dims)


def on_solver(body):
    pl.when(lax.axis_index("dp") % CORES == SOLVER)(body)


def first_gram_kernel(rows, damping_ref, one, two, left_ref, right_ref, damp_ref, stack):
    chip = lax.axis_index("dp") // CORES
    damp_ref[...] = jnp.full(damp_ref.shape, damping_ref[chip], jnp.float32)

    @on_solver
    def _():
        left_ref[...] = jnp.zeros_like(left_ref)
        right_ref[...] = jnp.zeros_like(right_ref)
        add_gram(rows, (one, two), left_ref, right_ref, stack)


def gram_kernel(rows, one, two, given_left, given_right, left_ref, right_ref, stack):
    @on_solver
    def _():
        left_ref[...] = given_left[...]
        right_ref[...] = given_right[...]
        add_gram(rows, (one, two), left_ref, right_ref, stack)


def gram(rows, pair, given=(), damping=None):
    width = pair[0].shape[1]
    half = width // 2
    shapes = [near((half, half)), near((width, half))]
    first = damping is not None
    return pl.pallas_call(
        functools.partial(first_gram_kernel if first else gram_kernel, rows),
        out_shape=shapes + [near((8, 128))] * first,
        in_specs=[SMEM] * first + [VMEM] * (2 + len(given)),
        out_specs=[VMEM] * (2 + first),
        scratch_shapes=[pltpu.VMEM((2 * rows, width), jnp.float32)],
        compiler_params=grant(16),
        cost_estimate=cost(0.6),
        name="gram",
    )(*([damping] * first), *hold(*pair, *given))


def solve_kernel(sizes, *refs):
    scores = refs[3 + CORES * sizes[0]]

    @pl.when(lax.axis_index("dp") % CORES != SOLVER)
    def _():
        scores[...] = jnp.zeros_like(scores)

    on_solver(functools.partial(solve_module, sizes, *refs))


def solve_module(sizes, *refs):
    chips, rows, per_device, groups, total_rows, scale = sizes
    refs = list(refs)
    damp_ref, left_ref, right_ref = refs[:3]
    blocks = [refs[3 + CORES * offset : 3 + CORES * (offset + 1)] for offset in range(chips)]
    scores, left, right, stack, state, high, low, asked = refs[3 + CORES * chips :]
    half = left_ref.shape[0]
    width = 2 * half
    chip = lax.axis_index("dp") // CORES
    pair = CORES * per_device
    total_queries = chips * pair
    group = total_queries // groups
    group_here = lax.axis_index("mod")

    for offset in range(chips):
        source = lax.bitwise_xor(chip, jnp.int32(offset))
        asked[pl.ds(pl.multiple_of(source * pair, pair), pair)] = jnp.concatenate(
            [block[rows : rows + per_device] for block in blocks[offset]], 0
        )

    left[...] = left_ref[...]
    right[...] = right_ref[...]
    add_gram(rows, [block[1 - SOLVER] for block in blocks[-2:]], left, right, stack)

    diagonal = lax.broadcasted_iota(jnp.int32, (half, half), 0) == lax.broadcasted_iota(
        jnp.int32, (half, half), 1
    )
    eye = diagonal.astype(jnp.float32)
    first, cross, last = left[...], right[0:half], right[half:]
    trace = jnp.sum((first + last) * eye, keepdims=True).reshape(1, 1)
    shift = (damp_ref[0:1, 0:1] * trace * (1.0 / width)) * eye
    first = first + shift
    last = last + shift
    squares = first * first + last * last + 2.0 * (cross * cross)
    squares = jnp.sum(squares, keepdims=True).reshape(1, 1) * (1.0 / total_rows**2)
    inverse_norm = lax.rsqrt(squares + epsilon)
    per_row = inverse_norm * (1.0 / total_rows)
    cross = cross * per_row
    state[0:half, 0:half] = first * per_row
    state[0:half, half:] = cross
    state[half:width, 0:half] = cross.T
    state[half:width, half:] = last * per_row
    for offset in range(groups):
        source = lax.bitwise_xor(group_here, jnp.int32(offset))
        state[width + offset * group : width + (offset + 1) * group] = (
            asked[pl.ds(pl.multiple_of(source * group, group), group)] * inverse_norm
        )

    for _ in range(SQUARINGS):
        high[...], low[...] = halves(state[...])

        def part(start, stop, column):
            columns = slice(column, column + half)
            return product_3(
                high[start:stop],
                low[start:stop],
                high[0:width, columns],
                low[0:width, columns],
            )

        state[0:half, 0:half] = 2.0 * state[0:half, 0:half] - part(0, half, 0)
        new = 2.0 * state[0:width, half:] - part(0, width, half)
        state[0:width, half:] = new
        state[half:width, 0:half] = new[0:half].T
        state[width:, 0:half] = 2.0 * state[width:, 0:half] - part(width, width + total_queries, 0)
        state[width:, half:] = 2.0 * state[width:, half:] - part(width, width + total_queries, half)

    high[...], low[...] = halves(state[...])
    asked_last = state[width:]
    conditioned = asked_last
    for _ in range(2 ** (NEWTON_STEPS - SQUARINGS) - 1):
        moved = narrow_product(conditioned, high[0:width], low[0:width])
        conditioned = asked_last + (conditioned - moved)
    conditioned = conditioned * scale
    for offset in range(chips):
        for place, block in enumerate(blocks[offset]):
            stack[place * rows : (place + 1) * rows] = block[0:rows]
        rows_high, rows_low = halves(stack[...])
        scores[offset * total_queries : (offset + 1) * total_queries] = narrow_product(
            conditioned, rows_high, rows_low, (((1,), (1,)), ((), ()))
        )


def solve(sizes, damp, given, blocks):
    chips, rows, per_device = sizes[:3]
    width = blocks[0].shape[1]
    half = width // 2
    total_queries = chips * CORES * per_device
    return pl.pallas_call(
        functools.partial(solve_kernel, sizes),
        out_shape=near((chips * total_queries, CORES * rows)),
        in_specs=[VMEM] * (3 + CORES * chips),
        out_specs=VMEM,
        scratch_shapes=[
            pltpu.VMEM((half, half), jnp.float32),
            pltpu.VMEM((width, half), jnp.float32),
            pltpu.VMEM((CORES * rows, width), jnp.float32),
            pltpu.VMEM((width + total_queries, width), jnp.float32),
            pltpu.VMEM((width + total_queries, width), jnp.bfloat16),
            pltpu.VMEM((width + total_queries, width), jnp.bfloat16),
            pltpu.VMEM((total_queries, width), jnp.float32),
        ],
        compiler_params=grant(24),
        cost_estimate=cost(9.0),
        name="solve",
    )(*hold(damp, *given, *blocks))


def swap(value):
    return lax.ppermute(value, "dp", [(i, i ^ 1) for i in range(lax.axis_size("dp"))])


def route(value, to_solver, others):
    devices, groups = lax.axis_size("dp"), lax.axis_size("mod")
    pairs = []
    for group in range(groups):
        for device in range(devices):
            goal = to_solver(group, device)
            if goal is None:
                goal = others(group, device)
            pairs.append((group * devices + device, goal[0] * devices + goal[1]))
    return lax.ppermute(value, ("mod", "dp"), pairs)


def same_core(value, offset):
    return route(
        value,
        lambda group, device: (group, device ^ (CORES * offset)) if device % CORES == SOLVER else None,
        lambda group, device: (group ^ 1, device),
    )


def cross_core(value, offset):
    return route(
        value,
        lambda group, device: None
        if device % CORES == SOLVER
        else (group, (device ^ (CORES * offset)) ^ 1),
        lambda group, device: (group, device ^ 1),
    )


def hand_over(value, active, axis, offset):
    move = CORES * offset

    def goal(group, device):
        if device % CORES != active:
            return None
        return (group ^ offset, device ^ 1) if axis == "mod" else (group, device ^ move ^ 1)

    return route(value, goal, lambda group, device: (group, device ^ 1))


def halvings(chips, groups):
    steps = []
    for axis, count in (("dp", chips), ("mod", groups)):
        while count > 1:
            count //= 2
            steps.append((axis, count))
    return steps


def sequence(chips):
    steps = []
    for first in range(1, chips, 2):
        offsets = range(first, min(first + 2, chips))
        steps += [("same", offset) for offset in offsets]
        steps += [("cross", offset) for offset in offsets]
    return steps + [("cross", 0)]


def influence(train_grads, queries, damping):
    rows, modules, width = train_grads.shape
    devices = lax.axis_size("dp")
    groups = lax.axis_size("mod")
    chips = devices // CORES
    packed = pack(train_grads, queries)
    arrived = {("same", 0): packed[0]}
    for kind, offset in sequence(chips):
        mover = same_core if kind == "same" else cross_core
        arrived[kind, offset] = mover(packed[offset], offset)
    blocks = [[arrived["cross", offset], arrived["same", offset]] for offset in range(chips)]
    *given, damp = gram(rows, blocks[0], damping=damping)
    for offset in range(1, chips - 2):
        given = gram(rows, blocks[offset], given)
    given = gram(rows, [block[SOLVER] for block in blocks[-2:]], given)
    sizes = (
        chips,
        rows,
        queries.shape[0],
        groups,
        rows * devices,
        1.0 / math.sqrt(modules * groups * width),
    )
    scores = solve(sizes, damp, given, sum(blocks, []))
    total, active = scores, SOLVER
    for axis, offset in halvings(chips, groups):
        keep = total.shape[0] // 2
        theirs = hand_over(total[keep:], active, axis, offset)
        total = swap(total[:keep]) + theirs
        active = 1 - active
    lanes = [total[:, core * rows : (core + 1) * rows] for core in range(CORES)]
    handed = swap(lanes[1 - active])
    return jnp.where(lax.axis_index("dp") % CORES == active, lanes[active], handed).T


def solution(mesh):
    return jax.shard_map(
        influence,
        mesh=mesh,
        in_specs=(P("dp", "mod", None), P("dp", "mod", None), P("mod")),
        out_specs=P("dp", "mod"),
        check_vma=False,
    )
```

```python
import functools
import math

import jax
import jax.numpy as jnp
from jax import lax
from jax.experimental import pallas as pl
from jax.experimental.pallas import tpu as pltpu
from jax.sharding import PartitionSpec as P


NEWTON_STEPS = 8
SQUARINGS = 6
CORES = 2
SOLVER = 1
PIECES = 4

epsilon = 1e-06

VMEM = pl.BlockSpec(memory_space=pltpu.VMEM)
SMEM = pl.BlockSpec(memory_space=pltpu.SMEM)
HBM = pl.BlockSpec(memory_space=pltpu.HBM)


def near(shape):
    return pltpu.VMEM(shape, jnp.float32)


def hold(*values):
    return [pltpu.with_memory_space_constraint(value, pltpu.VMEM) for value in values]


def grant(mebibytes):
    return pltpu.CompilerParams(vmem_limit_bytes=mebibytes << 20)


def cost(microseconds):
    return pl.CostEstimate(flops=int(microseconds * 1e9), bytes_accessed=0, transcendentals=0)


def halves(value):
    high = value.astype(jnp.bfloat16)
    return high, (value - high.astype(jnp.float32)).astype(jnp.bfloat16)


def product(left, right, dims=(((1,), (0,)), ((), ()))):
    return lax.dot_general(left, right, dims, preferred_element_type=jnp.float32)


def product_3(left_high, left_low, right_high, right_low, dims=(((1,), (0,)), ((), ()))):
    return (
        product(left_high, right_high, dims)
        + product(left_high, right_low, dims)
        + product(left_low, right_high, dims)
    )


def narrow_product(left, right_high, right_low, dims=(((1,), (0,)), ((), ()))):
    high, low = halves(left)
    count = left.shape[0]
    both = product(jnp.concatenate([high, low], 0), right_high, dims)
    return both[:count] + both[count:] + product(high, right_low, dims)


def pack_kernel(rows_ref, queries_ref, *refs):
    rows, queries, row_sems, query_sem = refs[-4:]
    blocks = refs[:-4]
    chip = lax.axis_index("dp") // CORES
    total = rows_ref.shape[0]
    step = total // PIECES
    query_copy = pltpu.make_async_copy(queries_ref, queries, query_sem)
    copies = [
        pltpu.make_async_copy(
            rows_ref.at[pl.ds(piece * step, step)],
            rows.at[pl.ds(piece * step, step)],
            row_sems.at[piece],
        )
        for piece in range(PIECES)
    ]
    for copy in copies:
        copy.start()
    query_copy.start()
    modules = [lax.bitwise_xor(chip, jnp.int32(offset)) for offset in range(len(blocks))]
    for piece, copy in enumerate(copies):
        copy.wait()
        here = slice(piece * step, (piece + 1) * step)
        for module, block in zip(modules, blocks):
            block[here] = rows[here, module, :]
    query_copy.wait()
    for module, block in zip(modules, blocks):
        block[total:] = queries[:, module, :]


def pack(train_grads, queries):
    rows, modules, width = train_grads.shape
    return pl.pallas_call(
        pack_kernel,
        out_shape=[near((rows + queries.shape[0], width))] * modules,
        in_specs=[HBM, HBM],
        out_specs=[VMEM] * modules,
        scratch_shapes=[
            pltpu.VMEM(train_grads.shape, jnp.float32),
            pltpu.VMEM(queries.shape, jnp.float32),
            pltpu.SemaphoreType.DMA((PIECES,)),
            pltpu.SemaphoreType.DMA,
        ],
        compiler_params=grant(16),
        cost_estimate=cost(1.5),
        name="pack",
    )(*(pltpu.with_memory_space_constraint(value, pltpu.HBM) for value in (train_grads, queries)))


def add_gram(rows, blocks, left_ref, right_ref, stack):
    half = left_ref.shape[0]
    for place, block in enumerate(blocks):
        stack[place * rows : (place + 1) * rows] = block[0:rows]
    high, low = halves(stack[...])
    dims = (((0,), (0,)), ((), ()))
    left_ref[...] += product_3(high[:, :half], low[:, :half], high[:, :half], low[:, :half], dims)
    right_ref[...] += product_3(high, low, high[:, half:], low[:, half:], dims)


def on_solver(body):
    pl.when(lax.axis_index("dp") % CORES == SOLVER)(body)


def first_gram_kernel(rows, damping_ref, one, two, left_ref, right_ref, damp_ref, stack):
    chip = lax.axis_index("dp") // CORES
    damp_ref[...] = jnp.full(damp_ref.shape, damping_ref[chip], jnp.float32)

    @on_solver
    def _():
        left_ref[...] = jnp.zeros_like(left_ref)
        right_ref[...] = jnp.zeros_like(right_ref)
        add_gram(rows, (one, two), left_ref, right_ref, stack)


def gram_kernel(rows, one, two, given_left, given_right, left_ref, right_ref, stack):
    @on_solver
    def _():
        left_ref[...] = given_left[...]
        right_ref[...] = given_right[...]
        add_gram(rows, (one, two), left_ref, right_ref, stack)


def gram(rows, pair, given=(), damping=None):
    width = pair[0].shape[1]
    half = width // 2
    shapes = [near((half, half)), near((width, half))]
    first = damping is not None
    return pl.pallas_call(
        functools.partial(first_gram_kernel if first else gram_kernel, rows),
        out_shape=shapes + [near((8, 128))] * first,
        in_specs=[SMEM] * first + [VMEM] * (2 + len(given)),
        out_specs=[VMEM] * (2 + first),
        scratch_shapes=[pltpu.VMEM((2 * rows, width), jnp.float32)],
        compiler_params=grant(16),
        cost_estimate=cost(0.6),
        name="gram",
    )(*([damping] * first), *hold(*pair, *given))


def solve_kernel(sizes, *refs):
    chips = sizes[0]
    scores = refs[3 + CORES * chips : 3 + (CORES + 1) * chips]

    @pl.when(lax.axis_index("dp") % CORES != SOLVER)
    def _():
        for score in scores:
            score[...] = jnp.zeros_like(score)

    on_solver(functools.partial(solve_module, sizes, *refs))


def solve_module(sizes, *refs):
    chips, rows, per_device, groups, total_rows, scale = sizes
    refs = list(refs)
    damp_ref, left_ref, right_ref = refs[:3]
    blocks = [refs[3 + CORES * offset : 3 + CORES * (offset + 1)] for offset in range(chips)]
    scores = refs[3 + CORES * chips : 3 + (CORES + 1) * chips]
    left, right, stack, state, high, low, asked = refs[3 + (CORES + 1) * chips :]
    half = left_ref.shape[0]
    width = 2 * half
    chip = lax.axis_index("dp") // CORES
    pair = CORES * per_device
    total_queries = chips * pair
    group = total_queries // groups
    group_here = lax.axis_index("mod")

    for offset in range(chips):
        source = lax.bitwise_xor(chip, jnp.int32(offset))
        asked[pl.ds(pl.multiple_of(source * pair, pair), pair)] = jnp.concatenate(
            [block[rows : rows + per_device] for block in blocks[offset]], 0
        )

    left[...] = left_ref[...]
    right[...] = right_ref[...]
    add_gram(rows, [block[1 - SOLVER] for block in blocks[-2:]], left, right, stack)

    diagonal = lax.broadcasted_iota(jnp.int32, (half, half), 0) == lax.broadcasted_iota(
        jnp.int32, (half, half), 1
    )
    eye = diagonal.astype(jnp.float32)
    first, cross, last = left[...], right[0:half], right[half:]
    trace = jnp.sum((first + last) * eye, keepdims=True).reshape(1, 1)
    shift = (damp_ref[0:1, 0:1] * trace * (1.0 / width)) * eye
    first = first + shift
    last = last + shift
    squares = first * first + last * last + 2.0 * (cross * cross)
    squares = jnp.sum(squares, keepdims=True).reshape(1, 1) * (1.0 / total_rows**2)
    inverse_norm = lax.rsqrt(squares + epsilon)
    per_row = inverse_norm * (1.0 / total_rows)
    cross = cross * per_row
    state[0:half, 0:half] = first * per_row
    state[0:half, half:] = cross
    state[half:width, 0:half] = cross.T
    state[half:width, half:] = last * per_row
    for offset in range(groups):
        source = lax.bitwise_xor(group_here, jnp.int32(offset))
        state[width + offset * group : width + (offset + 1) * group] = (
            asked[pl.ds(pl.multiple_of(source * group, group), group)] * inverse_norm
        )

    for _ in range(SQUARINGS):
        high[...], low[...] = halves(state[...])

        def part(start, stop, column):
            columns = slice(column, column + half)
            return product_3(
                high[start:stop],
                low[start:stop],
                high[0:width, columns],
                low[0:width, columns],
            )

        state[0:half, 0:half] = 2.0 * state[0:half, 0:half] - part(0, half, 0)
        new = 2.0 * state[0:width, half:] - part(0, width, half)
        state[0:width, half:] = new
        state[half:width, 0:half] = new[0:half].T
        state[width:, 0:half] = 2.0 * state[width:, 0:half] - part(width, width + total_queries, 0)
        state[width:, half:] = 2.0 * state[width:, half:] - part(width, width + total_queries, half)

    high[...], low[...] = halves(state[...])
    asked_last = state[width:]
    conditioned = asked_last
    for _ in range(2 ** (NEWTON_STEPS - SQUARINGS) - 1):
        moved = narrow_product(conditioned, high[0:width], low[0:width])
        conditioned = asked_last + (conditioned - moved)
    conditioned = conditioned * scale
    for offset in range(chips):
        for place, block in enumerate(blocks[offset]):
            stack[place * rows : (place + 1) * rows] = block[0:rows]
        rows_high, rows_low = halves(stack[...])
        scores[offset][...] = narrow_product(
            conditioned, rows_high, rows_low, (((1,), (1,)), ((), ()))
        )


def solve(sizes, damp, given, blocks):
    chips, rows, per_device = sizes[:3]
    width = blocks[0].shape[1]
    half = width // 2
    total_queries = chips * CORES * per_device
    return pl.pallas_call(
        functools.partial(solve_kernel, sizes),
        out_shape=[near((total_queries, CORES * rows))] * chips,
        in_specs=[VMEM] * (3 + CORES * chips),
        out_specs=[VMEM] * chips,
        scratch_shapes=[
            pltpu.VMEM((half, half), jnp.float32),
            pltpu.VMEM((width, half), jnp.float32),
            pltpu.VMEM((CORES * rows, width), jnp.float32),
            pltpu.VMEM((width + total_queries, width), jnp.float32),
            pltpu.VMEM((width + total_queries, width), jnp.bfloat16),
            pltpu.VMEM((width + total_queries, width), jnp.bfloat16),
            pltpu.VMEM((total_queries, width), jnp.float32),
        ],
        compiler_params=grant(24),
        cost_estimate=cost(9.0),
        name="solve",
    )(*hold(damp, *given, *blocks))


def swap(value, axis, offset):
    return lax.ppermute(value, axis, [(i, i ^ offset) for i in range(lax.axis_size(axis))])


def route(value, to_solver, others):
    devices, groups = lax.axis_size("dp"), lax.axis_size("mod")
    pairs = []
    for group in range(groups):
        for device in range(devices):
            goal = to_solver(group, device)
            if goal is None:
                goal = others(group, device)
            pairs.append((group * devices + device, goal[0] * devices + goal[1]))
    return lax.ppermute(value, ("mod", "dp"), pairs)


def same_core(value, offset):
    return route(
        value,
        lambda group, device: (group, device ^ (CORES * offset)) if device % CORES == SOLVER else None,
        lambda group, device: (group ^ 1, device),
    )


def cross_core(value, offset):
    return route(
        value,
        lambda group, device: None
        if device % CORES == SOLVER
        else (group, (device ^ (CORES * offset)) ^ 1),
        lambda group, device: (group, device ^ 1),
    )


def sequence(chips):
    steps = []
    for first in range(1, chips, 2):
        offsets = range(first, min(first + 2, chips))
        steps += [("same", offset) for offset in offsets]
        steps += [("cross", offset) for offset in offsets]
    return steps + [("cross", 0)]


def influence(train_grads, queries, damping):
    rows, modules, width = train_grads.shape
    devices = lax.axis_size("dp")
    groups = lax.axis_size("mod")
    chips = devices // CORES
    packed = pack(train_grads, queries)
    arrived = {("same", 0): packed[0]}
    for kind, offset in sequence(chips):
        mover = same_core if kind == "same" else cross_core
        arrived[kind, offset] = mover(packed[offset], offset)
    blocks = [[arrived["cross", offset], arrived["same", offset]] for offset in range(chips)]
    *given, damp = gram(rows, blocks[0], damping=damping)
    for offset in range(1, chips - 2):
        given = gram(rows, blocks[offset], given)
    given = gram(rows, [block[SOLVER] for block in blocks[-2:]], given)
    sizes = (
        chips,
        rows,
        queries.shape[0],
        groups,
        rows * devices,
        1.0 / math.sqrt(modules * groups * width),
    )
    scores = solve(sizes, damp, given, sum(blocks, []))
    total = scores[0]
    for offset in range(chips - 1, 0, -1):
        total = total + swap(scores[offset], "dp", CORES * offset)
    bit = groups // 2
    while bit:
        keep = total.shape[0] // 2
        total = total[:keep] + swap(total[keep:], "mod", bit)
        bit //= 2
    solver = lax.axis_index("dp") % CORES == SOLVER
    result = jnp.where(solver, total[:, SOLVER * rows :], swap(total[:, :rows], "dp", 1))
    return result.T


def solution(mesh):
    return jax.shard_map(
        influence,
        mesh=mesh,
        in_specs=(P("dp", "mod", None), P("dp", "mod", None), P("mod")),
        out_specs=P("dp", "mod"),
        check_vma=False,
    )
```

```python
import functools
import math

import jax
import jax.numpy as jnp
from jax import lax
from jax.experimental import pallas as pl
from jax.experimental.pallas import tpu as pltpu
from jax.sharding import PartitionSpec as P


NEWTON_STEPS = 8
SQUARINGS = 6
CORES = 2
SOLVER = 1
PIECES = 4

epsilon = 1e-06

VMEM = pl.BlockSpec(memory_space=pltpu.VMEM)
SMEM = pl.BlockSpec(memory_space=pltpu.SMEM)
HBM = pl.BlockSpec(memory_space=pltpu.HBM)


def near(shape):
    return pltpu.VMEM(shape, jnp.float32)


def hold(*values):
    return [pltpu.with_memory_space_constraint(value, pltpu.VMEM) for value in values]


def grant(mebibytes):
    return pltpu.CompilerParams(vmem_limit_bytes=mebibytes << 20)


def cost(microseconds):
    return pl.CostEstimate(flops=int(microseconds * 1e9), bytes_accessed=0, transcendentals=0)


def halves(value):
    high = value.astype(jnp.bfloat16)
    return high, (value - high.astype(jnp.float32)).astype(jnp.bfloat16)


def product(left, right, dims=(((1,), (0,)), ((), ()))):
    return lax.dot_general(left, right, dims, preferred_element_type=jnp.float32)


def product_3(left_high, left_low, right_high, right_low, dims=(((1,), (0,)), ((), ()))):
    return (
        product(left_high, right_high, dims)
        + product(left_high, right_low, dims)
        + product(left_low, right_high, dims)
    )


def narrow_product(left, right_high, right_low, dims=(((1,), (0,)), ((), ()))):
    high, low = halves(left)
    count = left.shape[0]
    both = product(jnp.concatenate([high, low], 0), right_high, dims)
    return both[:count] + both[count:] + product(high, right_low, dims)


def pack_kernel(rows_ref, queries_ref, *refs):
    rows, queries, row_sems, query_sem = refs[-4:]
    blocks = refs[:-4]
    chip = lax.axis_index("dp") // CORES
    total = rows_ref.shape[0]
    step = total // PIECES
    query_copy = pltpu.make_async_copy(queries_ref, queries, query_sem)
    copies = [
        pltpu.make_async_copy(
            rows_ref.at[pl.ds(piece * step, step)],
            rows.at[pl.ds(piece * step, step)],
            row_sems.at[piece],
        )
        for piece in range(PIECES)
    ]
    for copy in copies:
        copy.start()
    query_copy.start()
    modules = [lax.bitwise_xor(chip, jnp.int32(offset)) for offset in range(len(blocks))]
    for piece, copy in enumerate(copies):
        copy.wait()
        here = slice(piece * step, (piece + 1) * step)
        for module, block in zip(modules, blocks):
            block[here] = rows[here, module, :]
    query_copy.wait()
    for module, block in zip(modules, blocks):
        block[total:] = queries[:, module, :]


def pack(train_grads, queries):
    rows, modules, width = train_grads.shape
    return pl.pallas_call(
        pack_kernel,
        out_shape=[near((rows + queries.shape[0], width))] * modules,
        in_specs=[HBM, HBM],
        out_specs=[VMEM] * modules,
        scratch_shapes=[
            pltpu.VMEM(train_grads.shape, jnp.float32),
            pltpu.VMEM(queries.shape, jnp.float32),
            pltpu.SemaphoreType.DMA((PIECES,)),
            pltpu.SemaphoreType.DMA,
        ],
        compiler_params=grant(16),
        cost_estimate=cost(1.5),
        name="pack",
    )(*(pltpu.with_memory_space_constraint(value, pltpu.HBM) for value in (train_grads, queries)))


def add_gram(rows, blocks, left_ref, right_ref, stack):
    half = left_ref.shape[0]
    for place, block in enumerate(blocks):
        stack[place * rows : (place + 1) * rows] = block[0:rows]
    high, low = halves(stack[...])
    dims = (((0,), (0,)), ((), ()))
    left_ref[...] += product_3(high[:, :half], low[:, :half], high[:, :half], low[:, :half], dims)
    right_ref[...] += product_3(high, low, high[:, half:], low[:, half:], dims)


def on_solver(body):
    pl.when(lax.axis_index("dp") % CORES == SOLVER)(body)


def first_gram_kernel(rows, damping_ref, one, two, left_ref, right_ref, damp_ref, stack):
    chip = lax.axis_index("dp") // CORES
    damp_ref[...] = jnp.full(damp_ref.shape, damping_ref[chip], jnp.float32)

    @on_solver
    def _():
        left_ref[...] = jnp.zeros_like(left_ref)
        right_ref[...] = jnp.zeros_like(right_ref)
        add_gram(rows, (one, two), left_ref, right_ref, stack)


def gram_kernel(rows, one, two, given_left, given_right, left_ref, right_ref, stack):
    @on_solver
    def _():
        left_ref[...] = given_left[...]
        right_ref[...] = given_right[...]
        add_gram(rows, (one, two), left_ref, right_ref, stack)


def gram(rows, pair, given=(), damping=None):
    width = pair[0].shape[1]
    half = width // 2
    shapes = [near((half, half)), near((width, half))]
    first = damping is not None
    return pl.pallas_call(
        functools.partial(first_gram_kernel if first else gram_kernel, rows),
        out_shape=shapes + [near((8, 128))] * first,
        in_specs=[SMEM] * first + [VMEM] * (2 + len(given)),
        out_specs=[VMEM] * (2 + first),
        scratch_shapes=[pltpu.VMEM((2 * rows, width), jnp.float32)],
        compiler_params=grant(16),
        cost_estimate=cost(0.6),
        name="gram",
    )(*([damping] * first), *hold(*pair, *given))


def solve_kernel(sizes, *refs):
    chips = sizes[0]
    scores = refs[3 + CORES * chips : 3 + (CORES + 1) * chips]

    @pl.when(lax.axis_index("dp") % CORES != SOLVER)
    def _():
        for score in scores:
            score[...] = jnp.zeros_like(score)

    on_solver(functools.partial(solve_module, sizes, *refs))


def solve_module(sizes, *refs):
    chips, rows, per_device, groups, total_rows, scale = sizes
    refs = list(refs)
    damp_ref, left_ref, right_ref = refs[:3]
    blocks = [refs[3 + CORES * offset : 3 + CORES * (offset + 1)] for offset in range(chips)]
    scores = refs[3 + CORES * chips : 3 + (CORES + 1) * chips]
    left, right, stack, state, high, low, asked = refs[3 + (CORES + 1) * chips :]
    half = left_ref.shape[0]
    width = 2 * half
    chip = lax.axis_index("dp") // CORES
    pair = CORES * per_device
    total_queries = chips * pair
    group = total_queries // groups
    group_here = lax.axis_index("mod")

    for offset in range(chips):
        source = lax.bitwise_xor(chip, jnp.int32(offset))
        asked[pl.ds(pl.multiple_of(source * pair, pair), pair)] = jnp.concatenate(
            [block[rows : rows + per_device] for block in blocks[offset]], 0
        )

    left[...] = left_ref[...]
    right[...] = right_ref[...]
    add_gram(rows, [block[1 - SOLVER] for block in blocks[-2:]], left, right, stack)

    diagonal = lax.broadcasted_iota(jnp.int32, (half, half), 0) == lax.broadcasted_iota(
        jnp.int32, (half, half), 1
    )
    eye = diagonal.astype(jnp.float32)
    first, cross, last = left[...], right[0:half], right[half:]
    trace = jnp.sum((first + last) * eye, keepdims=True).reshape(1, 1)
    shift = (damp_ref[0:1, 0:1] * trace * (1.0 / width)) * eye
    first = first + shift
    last = last + shift
    squares = first * first + last * last + 2.0 * (cross * cross)
    squares = jnp.sum(squares, keepdims=True).reshape(1, 1) * (1.0 / total_rows**2)
    inverse_norm = lax.rsqrt(squares + epsilon)
    per_row = inverse_norm * (1.0 / total_rows)
    cross = cross * per_row
    state[0:half, 0:half] = first * per_row
    state[0:half, half:] = cross
    state[half:width, 0:half] = cross.T
    state[half:width, half:] = last * per_row
    for offset in range(groups):
        source = lax.bitwise_xor(group_here, jnp.int32(offset))
        state[width + offset * group : width + (offset + 1) * group] = (
            asked[pl.ds(pl.multiple_of(source * group, group), group)] * inverse_norm
        )

    for _ in range(SQUARINGS):
        high[...], low[...] = halves(state[...])

        def part(start, stop, column):
            columns = slice(column, column + half)
            return product_3(
                high[start:stop],
                low[start:stop],
                high[0:width, columns],
                low[0:width, columns],
            )

        state[0:half, 0:half] = 2.0 * state[0:half, 0:half] - part(0, half, 0)
        new = 2.0 * state[0:width, half:] - part(0, width, half)
        state[0:width, half:] = new
        state[half:width, 0:half] = new[0:half].T
        state[width:, 0:half] = 2.0 * state[width:, 0:half] - part(width, width + total_queries, 0)
        state[width:, half:] = 2.0 * state[width:, half:] - part(width, width + total_queries, half)

    high[...], low[...] = halves(state[...])
    asked_last = state[width:]
    conditioned = asked_last
    for _ in range(2 ** (NEWTON_STEPS - SQUARINGS) - 1):
        moved = narrow_product(conditioned, high[0:width], low[0:width])
        conditioned = asked_last + (conditioned - moved)
    conditioned = conditioned * scale
    for offset in range(chips):
        for place, block in enumerate(blocks[offset]):
            stack[place * rows : (place + 1) * rows] = block[0:rows]
        rows_high, rows_low = halves(stack[...])
        scores[offset][...] = narrow_product(
            conditioned, rows_high, rows_low, (((1,), (1,)), ((), ()))
        )


def solve(sizes, damp, given, blocks):
    chips, rows, per_device = sizes[:3]
    width = blocks[0].shape[1]
    half = width // 2
    total_queries = chips * CORES * per_device
    return pl.pallas_call(
        functools.partial(solve_kernel, sizes),
        out_shape=[near((total_queries, CORES * rows))] * chips,
        in_specs=[VMEM] * (3 + CORES * chips),
        out_specs=[VMEM] * chips,
        scratch_shapes=[
            pltpu.VMEM((half, half), jnp.float32),
            pltpu.VMEM((width, half), jnp.float32),
            pltpu.VMEM((CORES * rows, width), jnp.float32),
            pltpu.VMEM((width + total_queries, width), jnp.float32),
            pltpu.VMEM((width + total_queries, width), jnp.bfloat16),
            pltpu.VMEM((width + total_queries, width), jnp.bfloat16),
            pltpu.VMEM((total_queries, width), jnp.float32),
        ],
        compiler_params=grant(24),
        cost_estimate=cost(9.0),
        name="solve",
    )(*hold(damp, *given, *blocks))


def swap(value, axis, offset):
    return lax.ppermute(value, axis, [(i, i ^ offset) for i in range(lax.axis_size(axis))])


def route(value, to_solver, others):
    devices, groups = lax.axis_size("dp"), lax.axis_size("mod")
    pairs = []
    for group in range(groups):
        for device in range(devices):
            goal = to_solver(group, device)
            if goal is None:
                goal = others(group, device)
            pairs.append((group * devices + device, goal[0] * devices + goal[1]))
    return lax.ppermute(value, ("mod", "dp"), pairs)


def same_core(value, offset):
    return route(
        value,
        lambda group, device: (group, device ^ (CORES * offset)) if device % CORES == SOLVER else None,
        lambda group, device: (group ^ 1, device),
    )


def cross_core(value, offset):
    return route(
        value,
        lambda group, device: None
        if device % CORES == SOLVER
        else (group, (device ^ (CORES * offset)) ^ 1),
        lambda group, device: (group, device ^ 1),
    )


def sequence(chips):
    same = [("same", offset) for offset in [chips - 1, *range(1, chips - 1)]]
    return same + [("cross", offset) for offset in range(1, chips)]


def influence(train_grads, queries, damping):
    rows, modules, width = train_grads.shape
    devices = lax.axis_size("dp")
    groups = lax.axis_size("mod")
    chips = devices // CORES
    packed = pack(train_grads, queries)
    arrived = {("same", 0): packed[0]}
    steps = sequence(chips)
    for kind, offset in steps + [("cross", 0)]:
        mover = same_core if kind == "same" else cross_core
        arrived[kind, offset] = mover(packed[offset], offset)
    blocks = [[arrived["cross", offset], arrived["same", offset]] for offset in range(chips)]
    *given, damp = gram(rows, blocks[0], damping=damping)
    for place in range(1, chips - 1):
        pair = [arrived[step] for step in steps[2 * place - 2 : 2 * place]]
        given = gram(rows, pair, given)
    sizes = (
        chips,
        rows,
        queries.shape[0],
        groups,
        rows * devices,
        1.0 / math.sqrt(modules * groups * width),
    )
    scores = solve(sizes, damp, given, sum(blocks, []))
    total = scores[0]
    for offset in range(chips - 1, 0, -1):
        total = total + swap(scores[offset], "dp", CORES * offset)
    bit = groups // 2
    while bit:
        keep = total.shape[0] // 2
        total = total[:keep] + swap(total[keep:], "mod", bit)
        bit //= 2
    solver = lax.axis_index("dp") % CORES == SOLVER
    result = jnp.where(solver, total[:, SOLVER * rows :], swap(total[:, :rows], "dp", 1))
    return result.T


def solution(mesh):
    return jax.shard_map(
        influence,
        mesh=mesh,
        in_specs=(P("dp", "mod", None), P("dp", "mod", None), P("mod")),
        out_specs=P("dp", "mod"),
        check_vma=False,
    )
```

```python
import functools
import math

import jax
import jax.numpy as jnp
from jax import lax
from jax.experimental import pallas as pl
from jax.experimental.pallas import tpu as pltpu
from jax.sharding import PartitionSpec as P


NEWTON_STEPS = 8
SQUARINGS = 6
CORES = 2
SOLVER = 1
PIECES = 4

epsilon = 1e-06

VMEM = pl.BlockSpec(memory_space=pltpu.VMEM)
SMEM = pl.BlockSpec(memory_space=pltpu.SMEM)
HBM = pl.BlockSpec(memory_space=pltpu.HBM)


def near(shape):
    return pltpu.VMEM(shape, jnp.float32)


def hold(*values):
    return [pltpu.with_memory_space_constraint(value, pltpu.VMEM) for value in values]


def grant(mebibytes):
    return pltpu.CompilerParams(vmem_limit_bytes=mebibytes << 20)


def cost(microseconds):
    return pl.CostEstimate(flops=int(microseconds * 1e9), bytes_accessed=0, transcendentals=0)


def halves(value):
    high = value.astype(jnp.bfloat16)
    return high, (value - high.astype(jnp.float32)).astype(jnp.bfloat16)


def product(left, right, dims=(((1,), (0,)), ((), ()))):
    return lax.dot_general(left, right, dims, preferred_element_type=jnp.float32)


def product_3(left_high, left_low, right_high, right_low, dims=(((1,), (0,)), ((), ()))):
    return (
        product(left_high, right_high, dims)
        + product(left_high, right_low, dims)
        + product(left_low, right_high, dims)
    )


def narrow_product(left, right_high, right_low, dims=(((1,), (0,)), ((), ()))):
    high, low = halves(left)
    count = left.shape[0]
    both = product(jnp.concatenate([high, low], 0), right_high, dims)
    return both[:count] + both[count:] + product(high, right_low, dims)


def pack_kernel(rows_ref, queries_ref, *refs):
    rows, queries, row_sems, query_sem = refs[-4:]
    blocks = refs[:-4]
    chip = lax.axis_index("dp") // CORES
    total = rows_ref.shape[0]
    step = total // PIECES
    query_copy = pltpu.make_async_copy(queries_ref, queries, query_sem)
    copies = [
        pltpu.make_async_copy(
            rows_ref.at[pl.ds(piece * step, step)],
            rows.at[pl.ds(piece * step, step)],
            row_sems.at[piece],
        )
        for piece in range(PIECES)
    ]
    for copy in copies:
        copy.start()
    query_copy.start()
    modules = [lax.bitwise_xor(chip, jnp.int32(offset)) for offset in range(len(blocks))]
    for piece, copy in enumerate(copies):
        copy.wait()
        here = slice(piece * step, (piece + 1) * step)
        for module, block in zip(modules, blocks):
            block[here] = rows[here, module, :]
    query_copy.wait()
    for module, block in zip(modules, blocks):
        block[total:] = queries[:, module, :]


def pack(train_grads, queries):
    rows, modules, width = train_grads.shape
    return pl.pallas_call(
        pack_kernel,
        out_shape=[near((rows + queries.shape[0], width))] * modules,
        in_specs=[HBM, HBM],
        out_specs=[VMEM] * modules,
        scratch_shapes=[
            pltpu.VMEM(train_grads.shape, jnp.float32),
            pltpu.VMEM(queries.shape, jnp.float32),
            pltpu.SemaphoreType.DMA((PIECES,)),
            pltpu.SemaphoreType.DMA,
        ],
        compiler_params=grant(16),
        cost_estimate=cost(1.5),
        name="pack",
    )(*(pltpu.with_memory_space_constraint(value, pltpu.HBM) for value in (train_grads, queries)))


def add_gram(rows, blocks, left_ref, right_ref, stack):
    half = left_ref.shape[0]
    for place, block in enumerate(blocks):
        stack[place * rows : (place + 1) * rows] = block[0:rows]
    high, low = halves(stack[...])
    dims = (((0,), (0,)), ((), ()))
    left_ref[...] += product_3(high[:, :half], low[:, :half], high[:, :half], low[:, :half], dims)
    right_ref[...] += product_3(high, low, high[:, half:], low[:, half:], dims)


def on_solver(body):
    pl.when(lax.axis_index("dp") % CORES == SOLVER)(body)


def first_gram_kernel(rows, damping_ref, one, two, left_ref, right_ref, damp_ref, stack):
    chip = lax.axis_index("dp") // CORES
    damp_ref[...] = jnp.full(damp_ref.shape, damping_ref[chip], jnp.float32)

    @on_solver
    def _():
        left_ref[...] = jnp.zeros_like(left_ref)
        right_ref[...] = jnp.zeros_like(right_ref)
        add_gram(rows, (one, two), left_ref, right_ref, stack)


def gram_kernel(rows, one, two, given_left, given_right, left_ref, right_ref, stack):
    @on_solver
    def _():
        left_ref[...] = given_left[...]
        right_ref[...] = given_right[...]
        add_gram(rows, (one, two), left_ref, right_ref, stack)


def gram(rows, pair, given=(), damping=None):
    width = pair[0].shape[1]
    half = width // 2
    shapes = [near((half, half)), near((width, half))]
    first = damping is not None
    return pl.pallas_call(
        functools.partial(first_gram_kernel if first else gram_kernel, rows),
        out_shape=shapes + [near((8, 128))] * first,
        in_specs=[SMEM] * first + [VMEM] * (2 + len(given)),
        out_specs=[VMEM] * (2 + first),
        scratch_shapes=[pltpu.VMEM((2 * rows, width), jnp.float32)],
        compiler_params=grant(16),
        cost_estimate=cost(0.6),
        name="gram",
    )(*([damping] * first), *hold(*pair, *given))


def solve_kernel(sizes, *refs):
    chips = sizes[0]
    scores = refs[3 + CORES * chips : 3 + (CORES + 1) * chips]

    @pl.when(lax.axis_index("dp") % CORES != SOLVER)
    def _():
        for score in scores:
            score[...] = jnp.zeros_like(score)

    on_solver(functools.partial(solve_module, sizes, *refs))


def solve_module(sizes, *refs):
    chips, rows, per_device, groups, total_rows, scale = sizes
    refs = list(refs)
    damp_ref, left_ref, right_ref = refs[:3]
    blocks = [refs[3 + CORES * offset : 3 + CORES * (offset + 1)] for offset in range(chips)]
    scores = refs[3 + CORES * chips : 3 + (CORES + 1) * chips]
    first_gram, right_gram, stack, state, high, low, asked = refs[3 + (CORES + 1) * chips :]
    half = left_ref.shape[0]
    width = 2 * half
    chip = lax.axis_index("dp") // CORES
    pair = CORES * per_device
    total_queries = chips * pair
    group = total_queries // groups
    group_here = lax.axis_index("mod")

    for offset in range(chips):
        source = lax.bitwise_xor(chip, jnp.int32(offset))
        asked[pl.ds(pl.multiple_of(source * pair, pair), pair)] = jnp.concatenate(
            [block[rows : rows + per_device] for block in blocks[offset]], 0
        )

    first_gram[...] = left_ref[...]
    right_gram[...] = right_ref[...]
    add_gram(rows, [block[1 - SOLVER] for block in blocks[-2:]], first_gram, right_gram, stack)

    diagonal = lax.broadcasted_iota(jnp.int32, (half, half), 0) == lax.broadcasted_iota(
        jnp.int32, (half, half), 1
    )
    eye = diagonal.astype(jnp.float32)
    first, cross, last = first_gram[...], right_gram[0:half], right_gram[half:]
    trace = jnp.sum((first + last) * eye, keepdims=True).reshape(1, 1)
    shift = (damp_ref[0:1, 0:1] * trace * (1.0 / width)) * eye
    first = first + shift
    last = last + shift
    squares = first * first + last * last + 2.0 * (cross * cross)
    squares = jnp.sum(squares, keepdims=True).reshape(1, 1) * (1.0 / total_rows**2)
    inverse_norm = lax.rsqrt(squares + epsilon)
    per_row = inverse_norm * (1.0 / total_rows)
    cross = cross * per_row
    state[0:half, 0:half] = first * per_row
    state[0:half, half:] = cross
    state[half:width, 0:half] = cross.T
    state[half:width, half:] = last * per_row
    for offset in range(groups):
        source = lax.bitwise_xor(group_here, jnp.int32(offset))
        state[width + offset * group : width + (offset + 1) * group] = (
            asked[pl.ds(pl.multiple_of(source * group, group), group)] * inverse_norm
        )

    for _ in range(SQUARINGS):
        high[...], low[...] = halves(state[...])
        high_left, high_right = high[0:width, 0:half], high[0:width, half:]
        low_left, low_right = low[0:width, 0:half], low[0:width, half:]
        mixed_left = product(high[0:width], low_left)
        mixed_right = product(high[0:width], low_right)
        right = product(high[0:width], high_right)
        left = product(high[0:half], high_left)
        new_first = 2.0 * state[0:half, 0:half] - (
            left + (mixed_left[0:half] + mixed_left[0:half].T)
        )
        new_cross = 2.0 * state[0:half, half:] - (
            right[0:half] + (mixed_right[0:half] + mixed_left[half:].T)
        )
        new_last = 2.0 * state[half:width, half:] - (
            right[half:] + (mixed_right[half:] + mixed_right[half:].T)
        )
        state[0:half, half:] = new_cross
        state[half:width, half:] = new_last
        state[half:width, 0:half] = state[0:half, half:].T
        asked_left = 2.0 * state[width:, 0:half] - product_3(
            high[width:], low[width:], high_left, low_left
        )
        asked_right = 2.0 * state[width:, half:] - product_3(
            high[width:], low[width:], high_right, low_right
        )
        state[0:half, 0:half] = new_first
        state[width:, 0:half] = asked_left
        state[width:, half:] = asked_right

    high[...], low[...] = halves(state[...])
    asked_last = state[width:]
    conditioned = asked_last
    for _ in range(2 ** (NEWTON_STEPS - SQUARINGS) - 1):
        moved = narrow_product(conditioned, high[0:width], low[0:width])
        conditioned = asked_last + (conditioned - moved)
    conditioned = conditioned * scale
    for offset in range(chips):
        for place, block in enumerate(blocks[offset]):
            stack[place * rows : (place + 1) * rows] = block[0:rows]
        rows_high, rows_low = halves(stack[...])
        scores[offset][...] = narrow_product(
            conditioned, rows_high, rows_low, (((1,), (1,)), ((), ()))
        )


def solve(sizes, damp, given, blocks):
    chips, rows, per_device = sizes[:3]
    width = blocks[0].shape[1]
    half = width // 2
    total_queries = chips * CORES * per_device
    return pl.pallas_call(
        functools.partial(solve_kernel, sizes),
        out_shape=[near((total_queries, CORES * rows))] * chips,
        in_specs=[VMEM] * (3 + CORES * chips),
        out_specs=[VMEM] * chips,
        scratch_shapes=[
            pltpu.VMEM((half, half), jnp.float32),
            pltpu.VMEM((width, half), jnp.float32),
            pltpu.VMEM((CORES * rows, width), jnp.float32),
            pltpu.VMEM((width + total_queries, width), jnp.float32),
            pltpu.VMEM((width + total_queries, width), jnp.bfloat16),
            pltpu.VMEM((width + total_queries, width), jnp.bfloat16),
            pltpu.VMEM((total_queries, width), jnp.float32),
        ],
        compiler_params=grant(24),
        cost_estimate=cost(9.0),
        name="solve",
    )(*hold(damp, *given, *blocks))


def swap(value, axis, offset):
    return lax.ppermute(value, axis, [(i, i ^ offset) for i in range(lax.axis_size(axis))])


def route(value, to_solver, others):
    devices, groups = lax.axis_size("dp"), lax.axis_size("mod")
    pairs = []
    for group in range(groups):
        for device in range(devices):
            goal = to_solver(group, device)
            if goal is None:
                goal = others(group, device)
            pairs.append((group * devices + device, goal[0] * devices + goal[1]))
    return lax.ppermute(value, ("mod", "dp"), pairs)


def same_core(value, offset):
    return route(
        value,
        lambda group, device: (group, device ^ (CORES * offset)) if device % CORES == SOLVER else None,
        lambda group, device: (group ^ 1, device),
    )


def cross_core(value, offset):
    return route(
        value,
        lambda group, device: None
        if device % CORES == SOLVER
        else (group, (device ^ (CORES * offset)) ^ 1),
        lambda group, device: (group, device ^ 1),
    )


def sequence(chips):
    steps = []
    for first in range(1, chips, 2):
        offsets = range(first, min(first + 2, chips))
        steps += [("same", offset) for offset in offsets]
        steps += [("cross", offset) for offset in offsets]
    return steps + [("cross", 0)]


def influence(train_grads, queries, damping):
    rows, modules, width = train_grads.shape
    devices = lax.axis_size("dp")
    groups = lax.axis_size("mod")
    chips = devices // CORES
    packed = pack(train_grads, queries)
    arrived = {("same", 0): packed[0]}
    for kind, offset in sequence(chips):
        mover = same_core if kind == "same" else cross_core
        arrived[kind, offset] = mover(packed[offset], offset)
    blocks = [[arrived["cross", offset], arrived["same", offset]] for offset in range(chips)]
    *given, damp = gram(rows, blocks[0], damping=damping)
    for offset in range(1, chips - 2):
        given = gram(rows, blocks[offset], given)
    given = gram(rows, [block[SOLVER] for block in blocks[-2:]], given)
    sizes = (
        chips,
        rows,
        queries.shape[0],
        groups,
        rows * devices,
        1.0 / math.sqrt(modules * groups * width),
    )
    scores = solve(sizes, damp, given, sum(blocks, []))
    total = scores[0]
    for offset in range(chips - 1, 0, -1):
        total = total + swap(scores[offset], "dp", CORES * offset)
    bit = groups // 2
    while bit:
        keep = total.shape[0] // 2
        total = total[:keep] + swap(total[keep:], "mod", bit)
        bit //= 2
    solver = lax.axis_index("dp") % CORES == SOLVER
    result = jnp.where(solver, total[:, SOLVER * rows :], swap(total[:, :rows], "dp", 1))
    return result.T


def solution(mesh):
    return jax.shard_map(
        influence,
        mesh=mesh,
        in_specs=(P("dp", "mod", None), P("dp", "mod", None), P("mod")),
        out_specs=P("dp", "mod"),
        check_vma=False,
    )
```

```python
import functools
import math

import jax
import jax.numpy as jnp
from jax import lax
from jax.experimental import pallas as pl
from jax.experimental.pallas import tpu as pltpu
from jax.sharding import PartitionSpec as P


NEWTON_STEPS = 8
SQUARINGS = 6
CORES = 2
SOLVER = 1
PIECES = 4

epsilon = 1e-06

VMEM = pl.BlockSpec(memory_space=pltpu.VMEM)
SMEM = pl.BlockSpec(memory_space=pltpu.SMEM)
HBM = pl.BlockSpec(memory_space=pltpu.HBM)


def near(shape):
    return pltpu.VMEM(shape, jnp.float32)


def hold(*values):
    return [pltpu.with_memory_space_constraint(value, pltpu.VMEM) for value in values]


def grant(mebibytes):
    return pltpu.CompilerParams(vmem_limit_bytes=mebibytes << 20)


def cost(microseconds):
    return pl.CostEstimate(flops=int(microseconds * 1e9), bytes_accessed=0, transcendentals=0)


def halves(value):
    high = value.astype(jnp.bfloat16)
    return high, (value - high.astype(jnp.float32)).astype(jnp.bfloat16)


def product(left, right, dims=(((1,), (0,)), ((), ()))):
    return lax.dot_general(left, right, dims, preferred_element_type=jnp.float32)


def product_3(left_high, left_low, right_high, right_low, dims=(((1,), (0,)), ((), ()))):
    return (
        product(left_high, right_high, dims)
        + product(left_high, right_low, dims)
        + product(left_low, right_high, dims)
    )


def stacked_product(high, both, right_high, right_low, dims=(((1,), (0,)), ((), ()))):
    count = high.shape[0]
    sums = product(both, right_high, dims)
    return sums[:count] + sums[count:] + product(high, right_low, dims)


def narrow_product(left, right_high, right_low, dims=(((1,), (0,)), ((), ()))):
    high, low = halves(left)
    return stacked_product(high, jnp.concatenate([high, low], 0), right_high, right_low, dims)


def pack_kernel(rows_ref, queries_ref, *refs):
    rows, queries, row_sems, query_sem = refs[-4:]
    blocks = refs[:-4]
    chip = lax.axis_index("dp") // CORES
    total = rows_ref.shape[0]
    step = total // PIECES
    query_copy = pltpu.make_async_copy(queries_ref, queries, query_sem)
    copies = [
        pltpu.make_async_copy(
            rows_ref.at[pl.ds(piece * step, step)],
            rows.at[pl.ds(piece * step, step)],
            row_sems.at[piece],
        )
        for piece in range(PIECES)
    ]
    for copy in copies:
        copy.start()
    query_copy.start()
    modules = [lax.bitwise_xor(chip, jnp.int32(offset)) for offset in range(len(blocks))]
    for piece, copy in enumerate(copies):
        copy.wait()
        here = slice(piece * step, (piece + 1) * step)
        for module, block in zip(modules, blocks):
            block[here] = rows[here, module, :]
    query_copy.wait()
    for module, block in zip(modules, blocks):
        block[total:] = queries[:, module, :]


def pack(train_grads, queries):
    rows, modules, width = train_grads.shape
    return pl.pallas_call(
        pack_kernel,
        out_shape=[near((rows + queries.shape[0], width))] * modules,
        in_specs=[HBM, HBM],
        out_specs=[VMEM] * modules,
        scratch_shapes=[
            pltpu.VMEM(train_grads.shape, jnp.float32),
            pltpu.VMEM(queries.shape, jnp.float32),
            pltpu.SemaphoreType.DMA((PIECES,)),
            pltpu.SemaphoreType.DMA,
        ],
        compiler_params=grant(16),
        cost_estimate=cost(1.5),
        name="pack",
    )(*(pltpu.with_memory_space_constraint(value, pltpu.HBM) for value in (train_grads, queries)))


def add_gram(rows, blocks, left_ref, right_ref, stack):
    half = left_ref.shape[0]
    for place, block in enumerate(blocks):
        stack[place * rows : (place + 1) * rows] = block[0:rows]
    high, low = halves(stack[...])
    dims = (((0,), (0,)), ((), ()))
    left_ref[...] += product_3(high[:, :half], low[:, :half], high[:, :half], low[:, :half], dims)
    right_ref[...] += product_3(high, low, high[:, half:], low[:, half:], dims)


def on_solver(body):
    pl.when(lax.axis_index("dp") % CORES == SOLVER)(body)


def first_gram_kernel(rows, damping_ref, one, two, left_ref, right_ref, damp_ref, stack):
    chip = lax.axis_index("dp") // CORES
    damp_ref[...] = jnp.full(damp_ref.shape, damping_ref[chip], jnp.float32)

    @on_solver
    def _():
        left_ref[...] = jnp.zeros_like(left_ref)
        right_ref[...] = jnp.zeros_like(right_ref)
        add_gram(rows, (one, two), left_ref, right_ref, stack)


def gram_kernel(rows, one, two, given_left, given_right, left_ref, right_ref, stack):
    @on_solver
    def _():
        left_ref[...] = given_left[...]
        right_ref[...] = given_right[...]
        add_gram(rows, (one, two), left_ref, right_ref, stack)


def gram(rows, pair, given=(), damping=None):
    width = pair[0].shape[1]
    half = width // 2
    shapes = [near((half, half)), near((width, half))]
    first = damping is not None
    return pl.pallas_call(
        functools.partial(first_gram_kernel if first else gram_kernel, rows),
        out_shape=shapes + [near((8, 128))] * first,
        in_specs=[SMEM] * first + [VMEM] * (2 + len(given)),
        out_specs=[VMEM] * (2 + first),
        scratch_shapes=[pltpu.VMEM((2 * rows, width), jnp.float32)],
        compiler_params=grant(16),
        cost_estimate=cost(0.6),
        name="gram",
    )(*([damping] * first), *hold(*pair, *given))


def solve_kernel(sizes, *refs):
    chips = sizes[0]
    scores = refs[3 + CORES * chips : 3 + (CORES + 1) * chips]

    @pl.when(lax.axis_index("dp") % CORES != SOLVER)
    def _():
        for score in scores:
            score[...] = jnp.zeros_like(score)

    on_solver(functools.partial(solve_module, sizes, *refs))


def solve_module(sizes, *refs):
    chips, rows, per_device, groups, total_rows, scale = sizes
    refs = list(refs)
    damp_ref, left_ref, right_ref = refs[:3]
    blocks = [refs[3 + CORES * offset : 3 + CORES * (offset + 1)] for offset in range(chips)]
    scores = refs[3 + CORES * chips : 3 + (CORES + 1) * chips]
    first_gram, right_gram, stack, state, high, low, asked = refs[3 + (CORES + 1) * chips :]
    half = left_ref.shape[0]
    width = 2 * half
    chip = lax.axis_index("dp") // CORES
    pair = CORES * per_device
    total_queries = chips * pair
    group = total_queries // groups
    group_here = lax.axis_index("mod")

    for offset in range(chips):
        source = lax.bitwise_xor(chip, jnp.int32(offset))
        asked[pl.ds(pl.multiple_of(source * pair, pair), pair)] = jnp.concatenate(
            [block[rows : rows + per_device] for block in blocks[offset]], 0
        )

    first_gram[...] = left_ref[...]
    right_gram[...] = right_ref[...]
    add_gram(rows, [block[1 - SOLVER] for block in blocks[-2:]], first_gram, right_gram, stack)

    diagonal = lax.broadcasted_iota(jnp.int32, (half, half), 0) == lax.broadcasted_iota(
        jnp.int32, (half, half), 1
    )
    eye = diagonal.astype(jnp.float32)
    first, cross, last = first_gram[...], right_gram[0:half], right_gram[half:]
    trace = jnp.sum((first + last) * eye, keepdims=True).reshape(1, 1)
    shift = (damp_ref[0:1, 0:1] * trace * (1.0 / width)) * eye
    first = first + shift
    last = last + shift
    squares = first * first + last * last + 2.0 * (cross * cross)
    squares = jnp.sum(squares, keepdims=True).reshape(1, 1) * (1.0 / total_rows**2)
    inverse_norm = lax.rsqrt(squares + epsilon)
    per_row = inverse_norm * (1.0 / total_rows)
    cross = cross * per_row
    state[0:half, 0:half] = first * per_row
    state[0:half, half:] = cross
    state[half:width, 0:half] = cross.T
    state[half:width, half:] = last * per_row
    for offset in range(groups):
        source = lax.bitwise_xor(group_here, jnp.int32(offset))
        state[width + offset * group : width + (offset + 1) * group] = (
            asked[pl.ds(pl.multiple_of(source * group, group), group)] * inverse_norm
        )

    for _ in range(SQUARINGS):
        high[...], low[...] = halves(state[...])
        high_left, high_right = high[0:width, 0:half], high[0:width, half:]
        low_left, low_right = low[0:width, 0:half], low[0:width, half:]
        both = jnp.concatenate([high[width:], low[width:]], 0)
        mixed_left = product(high[0:width], low_left)
        mixed_right = product(high[0:width], low_right)
        right = product(high[0:width], high_right)
        left = product(high[0:half], high_left)
        new_first = 2.0 * state[0:half, 0:half] - (
            left + (mixed_left[0:half] + mixed_left[0:half].T)
        )
        new_cross = 2.0 * state[0:half, half:] - (
            right[0:half] + (mixed_right[0:half] + mixed_left[half:].T)
        )
        new_last = 2.0 * state[half:width, half:] - (
            right[half:] + (mixed_right[half:] + mixed_right[half:].T)
        )
        state[0:half, half:] = new_cross
        state[half:width, half:] = new_last
        state[half:width, 0:half] = state[0:half, half:].T
        asked_left = 2.0 * state[width:, 0:half] - stacked_product(
            high[width:], both, high_left, low_left
        )
        asked_right = 2.0 * state[width:, half:] - stacked_product(
            high[width:], both, high_right, low_right
        )
        state[0:half, 0:half] = new_first
        state[width:, 0:half] = asked_left
        state[width:, half:] = asked_right

    high[...], low[...] = halves(state[...])
    asked_last = state[width:]
    conditioned = asked_last
    for _ in range(2 ** (NEWTON_STEPS - SQUARINGS) - 1):
        moved = narrow_product(conditioned, high[0:width], low[0:width])
        conditioned = asked_last + (conditioned - moved)
    conditioned = conditioned * scale
    for offset in range(chips):
        for place, block in enumerate(blocks[offset]):
            stack[place * rows : (place + 1) * rows] = block[0:rows]
        rows_high, rows_low = halves(stack[...])
        scores[offset][...] = narrow_product(
            conditioned, rows_high, rows_low, (((1,), (1,)), ((), ()))
        )


def solve(sizes, damp, given, blocks):
    chips, rows, per_device = sizes[:3]
    width = blocks[0].shape[1]
    half = width // 2
    total_queries = chips * CORES * per_device
    return pl.pallas_call(
        functools.partial(solve_kernel, sizes),
        out_shape=[near((total_queries, CORES * rows))] * chips,
        in_specs=[VMEM] * (3 + CORES * chips),
        out_specs=[VMEM] * chips,
        scratch_shapes=[
            pltpu.VMEM((half, half), jnp.float32),
            pltpu.VMEM((width, half), jnp.float32),
            pltpu.VMEM((CORES * rows, width), jnp.float32),
            pltpu.VMEM((width + total_queries, width), jnp.float32),
            pltpu.VMEM((width + total_queries, width), jnp.bfloat16),
            pltpu.VMEM((width + total_queries, width), jnp.bfloat16),
            pltpu.VMEM((total_queries, width), jnp.float32),
        ],
        compiler_params=grant(24),
        cost_estimate=cost(9.0),
        name="solve",
    )(*hold(damp, *given, *blocks))


def swap(value, axis, offset):
    return lax.ppermute(value, axis, [(i, i ^ offset) for i in range(lax.axis_size(axis))])


def route(value, to_solver, others):
    devices, groups = lax.axis_size("dp"), lax.axis_size("mod")
    pairs = []
    for group in range(groups):
        for device in range(devices):
            goal = to_solver(group, device)
            if goal is None:
                goal = others(group, device)
            pairs.append((group * devices + device, goal[0] * devices + goal[1]))
    return lax.ppermute(value, ("mod", "dp"), pairs)


def same_core(value, offset):
    return route(
        value,
        lambda group, device: (group, device ^ (CORES * offset)) if device % CORES == SOLVER else None,
        lambda group, device: (group ^ 1, device),
    )


def cross_core(value, offset):
    return route(
        value,
        lambda group, device: None
        if device % CORES == SOLVER
        else (group, (device ^ (CORES * offset)) ^ 1),
        lambda group, device: (group, device ^ 1),
    )


def sequence(chips):
    steps = []
    for first in range(1, chips, 2):
        offsets = range(first, min(first + 2, chips))
        steps += [("same", offset) for offset in offsets]
        steps += [("cross", offset) for offset in offsets]
    return steps + [("cross", 0)]


def influence(train_grads, queries, damping):
    rows, modules, width = train_grads.shape
    devices = lax.axis_size("dp")
    groups = lax.axis_size("mod")
    chips = devices // CORES
    packed = pack(train_grads, queries)
    arrived = {("same", 0): packed[0]}
    for kind, offset in sequence(chips):
        mover = same_core if kind == "same" else cross_core
        arrived[kind, offset] = mover(packed[offset], offset)
    blocks = [[arrived["cross", offset], arrived["same", offset]] for offset in range(chips)]
    *given, damp = gram(rows, blocks[0], damping=damping)
    for offset in range(1, chips - 2):
        given = gram(rows, blocks[offset], given)
    given = gram(rows, [block[SOLVER] for block in blocks[-2:]], given)
    sizes = (
        chips,
        rows,
        queries.shape[0],
        groups,
        rows * devices,
        1.0 / math.sqrt(modules * groups * width),
    )
    scores = solve(sizes, damp, given, sum(blocks, []))
    total = scores[0]
    for offset in range(chips - 1, 0, -1):
        total = total + swap(scores[offset], "dp", CORES * offset)
    bit = groups // 2
    while bit:
        keep = total.shape[0] // 2
        total = total[:keep] + swap(total[keep:], "mod", bit)
        bit //= 2
    solver = lax.axis_index("dp") % CORES == SOLVER
    result = jnp.where(solver, total[:, SOLVER * rows :], swap(total[:, :rows], "dp", 1))
    return result.T


def solution(mesh):
    return jax.shard_map(
        influence,
        mesh=mesh,
        in_specs=(P("dp", "mod", None), P("dp", "mod", None), P("mod")),
        out_specs=P("dp", "mod"),
        check_vma=False,
    )
```

```python
import functools
import math

import jax
import jax.numpy as jnp
from jax import lax
from jax.experimental import pallas as pl
from jax.experimental.pallas import tpu as pltpu
from jax.sharding import PartitionSpec as P


NEWTON_STEPS = 8
SQUARINGS = 6
CORES = 2
SOLVER = 1
PIECES = 4

epsilon = 1e-06

VMEM = pl.BlockSpec(memory_space=pltpu.VMEM)
SMEM = pl.BlockSpec(memory_space=pltpu.SMEM)
HBM = pl.BlockSpec(memory_space=pltpu.HBM)


def near(shape):
    return pltpu.VMEM(shape, jnp.float32)


def hold(*values):
    return [pltpu.with_memory_space_constraint(value, pltpu.VMEM) for value in values]


def grant(mebibytes):
    return pltpu.CompilerParams(vmem_limit_bytes=mebibytes << 20)


def cost(microseconds):
    return pl.CostEstimate(flops=int(microseconds * 1e9), bytes_accessed=0, transcendentals=0)


def halves(value):
    high = value.astype(jnp.bfloat16)
    return high, (value - high.astype(jnp.float32)).astype(jnp.bfloat16)


def product(left, right, dims=(((1,), (0,)), ((), ()))):
    return lax.dot_general(left, right, dims, preferred_element_type=jnp.float32)


def product_3(left_high, left_low, right_high, right_low, dims=(((1,), (0,)), ((), ()))):
    return (
        product(left_high, right_high, dims)
        + product(left_high, right_low, dims)
        + product(left_low, right_high, dims)
    )


def stacked_product(high, both, right_high, right_low, dims=(((1,), (0,)), ((), ()))):
    count = high.shape[0]
    sums = product(both, right_high, dims)
    return sums[:count] + sums[count:] + product(high, right_low, dims)


def narrow_product(left, right_high, right_low, dims=(((1,), (0,)), ((), ()))):
    high, low = halves(left)
    return stacked_product(high, jnp.concatenate([high, low], 0), right_high, right_low, dims)


def pack_kernel(rows_ref, queries_ref, *refs):
    rows, queries, row_sems, query_sem = refs[-4:]
    blocks = refs[:-4]
    chip = lax.axis_index("dp") // CORES
    total = rows_ref.shape[0]
    step = total // PIECES
    query_copy = pltpu.make_async_copy(queries_ref, queries, query_sem)
    copies = [
        pltpu.make_async_copy(
            rows_ref.at[pl.ds(piece * step, step)],
            rows.at[pl.ds(piece * step, step)],
            row_sems.at[piece],
        )
        for piece in range(PIECES)
    ]
    for copy in copies:
        copy.start()
    query_copy.start()
    modules = [lax.bitwise_xor(chip, jnp.int32(offset)) for offset in range(len(blocks))]
    for piece, copy in enumerate(copies):
        copy.wait()
        here = slice(piece * step, (piece + 1) * step)
        for module, block in zip(modules, blocks):
            block[here] = rows[here, module, :]
    query_copy.wait()
    for module, block in zip(modules, blocks):
        block[total:] = queries[:, module, :]


def pack(train_grads, queries):
    rows, modules, width = train_grads.shape
    return pl.pallas_call(
        pack_kernel,
        out_shape=[near((rows + queries.shape[0], width))] * modules,
        in_specs=[HBM, HBM],
        out_specs=[VMEM] * modules,
        scratch_shapes=[
            pltpu.VMEM(train_grads.shape, jnp.float32),
            pltpu.VMEM(queries.shape, jnp.float32),
            pltpu.SemaphoreType.DMA((PIECES,)),
            pltpu.SemaphoreType.DMA,
        ],
        compiler_params=grant(16),
        cost_estimate=cost(1.5),
        name="pack",
    )(*(pltpu.with_memory_space_constraint(value, pltpu.HBM) for value in (train_grads, queries)))


def add_gram(rows, blocks, left_ref, right_ref, stack):
    half = left_ref.shape[0]
    for place, block in enumerate(blocks):
        stack[place * rows : (place + 1) * rows] = block[0:rows]
    high, low = halves(stack[...])
    dims = (((0,), (0,)), ((), ()))
    left_ref[...] += product_3(high[:, :half], low[:, :half], high[:, :half], low[:, :half], dims)
    right_ref[...] += product_3(high, low, high[:, half:], low[:, half:], dims)


def on_solver(body):
    pl.when(lax.axis_index("dp") % CORES == SOLVER)(body)


def first_gram_kernel(rows, damping_ref, one, two, left_ref, right_ref, damp_ref, stack):
    chip = lax.axis_index("dp") // CORES
    damp_ref[...] = jnp.full(damp_ref.shape, damping_ref[chip], jnp.float32)

    @on_solver
    def _():
        left_ref[...] = jnp.zeros_like(left_ref)
        right_ref[...] = jnp.zeros_like(right_ref)
        add_gram(rows, (one, two), left_ref, right_ref, stack)


def gram_kernel(rows, one, two, given_left, given_right, left_ref, right_ref, stack):
    @on_solver
    def _():
        left_ref[...] = given_left[...]
        right_ref[...] = given_right[...]
        add_gram(rows, (one, two), left_ref, right_ref, stack)


def gram(rows, pair, given=(), damping=None):
    width = pair[0].shape[1]
    half = width // 2
    shapes = [near((half, half)), near((width, half))]
    first = damping is not None
    return pl.pallas_call(
        functools.partial(first_gram_kernel if first else gram_kernel, rows),
        out_shape=shapes + [near((8, 128))] * first,
        in_specs=[SMEM] * first + [VMEM] * (2 + len(given)),
        out_specs=[VMEM] * (2 + first),
        scratch_shapes=[pltpu.VMEM((2 * rows, width), jnp.float32)],
        compiler_params=grant(16),
        cost_estimate=cost(0.6),
        name="gram",
    )(*([damping] * first), *hold(*pair, *given))


def solve_kernel(sizes, *refs):
    chips = sizes[0]
    scores = refs[3 + CORES * chips : 3 + (CORES + 1) * chips]

    @pl.when(lax.axis_index("dp") % CORES != SOLVER)
    def _():
        for score in scores:
            score[...] = jnp.zeros_like(score)

    on_solver(functools.partial(solve_module, sizes, *refs))


def solve_module(sizes, *refs):
    chips, rows, per_device, groups, total_rows, scale = sizes
    refs = list(refs)
    damp_ref, left_ref, right_ref = refs[:3]
    blocks = [refs[3 + CORES * offset : 3 + CORES * (offset + 1)] for offset in range(chips)]
    scores = refs[3 + CORES * chips : 3 + (CORES + 1) * chips]
    first_gram, right_gram, stack, state, high, low, asked = refs[3 + (CORES + 1) * chips :]
    half = left_ref.shape[0]
    width = 2 * half
    chip = lax.axis_index("dp") // CORES
    pair = CORES * per_device
    total_queries = chips * pair
    group = total_queries // groups
    group_here = lax.axis_index("mod")

    for offset in range(chips):
        source = lax.bitwise_xor(chip, jnp.int32(offset))
        asked[pl.ds(pl.multiple_of(source * pair, pair), pair)] = jnp.concatenate(
            [block[rows : rows + per_device] for block in blocks[offset]], 0
        )

    first_gram[...] = left_ref[...]
    right_gram[...] = right_ref[...]
    add_gram(rows, [block[1 - SOLVER] for block in blocks[-2:]], first_gram, right_gram, stack)

    diagonal = lax.broadcasted_iota(jnp.int32, (half, half), 0) == lax.broadcasted_iota(
        jnp.int32, (half, half), 1
    )
    eye = diagonal.astype(jnp.float32)
    first, cross, last = first_gram[...], right_gram[0:half], right_gram[half:]
    trace = jnp.sum((first + last) * eye, keepdims=True).reshape(1, 1)
    squares = first * first + last * last + 2.0 * (cross * cross)
    squares = jnp.sum(squares, keepdims=True).reshape(1, 1)
    shift = damp_ref[0:1, 0:1] * trace * (1.0 / width)
    squares = squares + 2.0 * shift * trace + shift * shift * width
    first = first + shift * eye
    last = last + shift * eye
    inverse_norm = lax.rsqrt(squares * (1.0 / total_rows**2) + epsilon)
    per_row = inverse_norm * (1.0 / total_rows)
    cross = cross * per_row
    state[0:half, 0:half] = first * per_row
    state[0:half, half:] = cross
    state[half:width, 0:half] = cross.T
    state[half:width, half:] = last * per_row
    for offset in range(groups):
        source = lax.bitwise_xor(group_here, jnp.int32(offset))
        state[width + offset * group : width + (offset + 1) * group] = (
            asked[pl.ds(pl.multiple_of(source * group, group), group)] * inverse_norm
        )

    for _ in range(SQUARINGS):
        high[...], low[...] = halves(state[...])
        high_left, high_right = high[0:width, 0:half], high[0:width, half:]
        low_left, low_right = low[0:width, 0:half], low[0:width, half:]
        both = jnp.concatenate([high[width:], low[width:]], 0)
        mixed_left = product(high[0:width], low_left)
        mixed_right = product(high[0:width], low_right)
        right = product(high[0:width], high_right)
        left = product(high[0:half], high_left)
        new_first = 2.0 * state[0:half, 0:half] - (
            left + (mixed_left[0:half] + mixed_left[0:half].T)
        )
        new_cross = 2.0 * state[0:half, half:] - (
            right[0:half] + (mixed_right[0:half] + mixed_left[half:].T)
        )
        new_last = 2.0 * state[half:width, half:] - (
            right[half:] + (mixed_right[half:] + mixed_right[half:].T)
        )
        state[0:half, half:] = new_cross
        state[half:width, half:] = new_last
        state[half:width, 0:half] = state[0:half, half:].T
        asked_left = 2.0 * state[width:, 0:half] - stacked_product(
            high[width:], both, high_left, low_left
        )
        asked_right = 2.0 * state[width:, half:] - stacked_product(
            high[width:], both, high_right, low_right
        )
        state[0:half, 0:half] = new_first
        state[width:, 0:half] = asked_left
        state[width:, half:] = asked_right

    high[...], low[...] = halves(state[...])
    asked_last = state[width:]
    conditioned = asked_last
    for _ in range(2 ** (NEWTON_STEPS - SQUARINGS) - 1):
        moved = narrow_product(conditioned, high[0:width], low[0:width])
        conditioned = asked_last + (conditioned - moved)
    conditioned = conditioned * scale
    for offset in range(chips):
        for place, block in enumerate(blocks[offset]):
            stack[place * rows : (place + 1) * rows] = block[0:rows]
        rows_high, rows_low = halves(stack[...])
        scores[offset][...] = narrow_product(
            conditioned, rows_high, rows_low, (((1,), (1,)), ((), ()))
        )


def solve(sizes, damp, given, blocks):
    chips, rows, per_device = sizes[:3]
    width = blocks[0].shape[1]
    half = width // 2
    total_queries = chips * CORES * per_device
    return pl.pallas_call(
        functools.partial(solve_kernel, sizes),
        out_shape=[near((total_queries, CORES * rows))] * chips,
        in_specs=[VMEM] * (3 + CORES * chips),
        out_specs=[VMEM] * chips,
        scratch_shapes=[
            pltpu.VMEM((half, half), jnp.float32),
            pltpu.VMEM((width, half), jnp.float32),
            pltpu.VMEM((CORES * rows, width), jnp.float32),
            pltpu.VMEM((width + total_queries, width), jnp.float32),
            pltpu.VMEM((width + total_queries, width), jnp.bfloat16),
            pltpu.VMEM((width + total_queries, width), jnp.bfloat16),
            pltpu.VMEM((total_queries, width), jnp.float32),
        ],
        compiler_params=grant(24),
        cost_estimate=cost(9.0),
        name="solve",
    )(*hold(damp, *given, *blocks))


def swap(value, axis, offset):
    return lax.ppermute(value, axis, [(i, i ^ offset) for i in range(lax.axis_size(axis))])


def route(value, to_solver, others):
    devices, groups = lax.axis_size("dp"), lax.axis_size("mod")
    pairs = []
    for group in range(groups):
        for device in range(devices):
            goal = to_solver(group, device)
            if goal is None:
                goal = others(group, device)
            pairs.append((group * devices + device, goal[0] * devices + goal[1]))
    return lax.ppermute(value, ("mod", "dp"), pairs)


def same_core(value, offset):
    return route(
        value,
        lambda group, device: (group, device ^ (CORES * offset)) if device % CORES == SOLVER else None,
        lambda group, device: (group ^ 1, device),
    )


def cross_core(value, offset):
    return route(
        value,
        lambda group, device: None
        if device % CORES == SOLVER
        else (group, (device ^ (CORES * offset)) ^ 1),
        lambda group, device: (group, device ^ 1),
    )


def sequence(chips):
    steps = []
    for first in range(1, chips, 2):
        offsets = range(first, min(first + 2, chips))
        steps += [("same", offset) for offset in offsets]
        steps += [("cross", offset) for offset in offsets]
    return steps + [("cross", 0)]


def influence(train_grads, queries, damping):
    rows, modules, width = train_grads.shape
    devices = lax.axis_size("dp")
    groups = lax.axis_size("mod")
    chips = devices // CORES
    packed = pack(train_grads, queries)
    arrived = {("same", 0): packed[0]}
    for kind, offset in sequence(chips):
        mover = same_core if kind == "same" else cross_core
        arrived[kind, offset] = mover(packed[offset], offset)
    blocks = [[arrived["cross", offset], arrived["same", offset]] for offset in range(chips)]
    *given, damp = gram(rows, blocks[0], damping=damping)
    for offset in range(1, chips - 2):
        given = gram(rows, blocks[offset], given)
    given = gram(rows, [block[SOLVER] for block in blocks[-2:]], given)
    sizes = (
        chips,
        rows,
        queries.shape[0],
        groups,
        rows * devices,
        1.0 / math.sqrt(modules * groups * width),
    )
    scores = solve(sizes, damp, given, sum(blocks, []))
    total = scores[0]
    for offset in range(chips - 1, 0, -1):
        sent = swap(scores[offset], "dp", CORES * offset)
        total = total + sent
    bit = groups // 2
    while bit:
        keep = total.shape[0] // 2
        total = total[:keep] + swap(total[keep:], "mod", bit)
        bit //= 2
    solver = lax.axis_index("dp") % CORES == SOLVER
    result = jnp.where(solver, total[:, SOLVER * rows :], swap(total[:, :rows], "dp", 1))
    return result.T


def solution(mesh):
    return jax.shard_map(
        influence,
        mesh=mesh,
        in_specs=(P("dp", "mod", None), P("dp", "mod", None), P("mod")),
        out_specs=P("dp", "mod"),
        check_vma=False,
    )
```
